128 devices in a mesh: cache: 32 (over y, z, core), mp: 4 (over x).
Axes of the slice: x: 4, y: 4, z: 4, core: 2. Of those that a mesh axis runs over, the one named last changes fastest.
Arguments:
- tokens: bfloat16 [262144, 768], P(('cache', 'mp')), may hold values from -6 to 6
- w_in: bfloat16 [768, 3072], P(None, 'mp'), may hold values from -0.21875 to 0.21875
- w_out: bfloat16 [3072, 768], P('mp'), may hold values from -0.109375 to 0.109375
- gain_in: float32 [768], replicated, may hold values from 0.1 to 1.9
- gain_out: float32 [768], replicated, may hold values from 0.1 to 1.9
- stale_cache: bfloat16 [131072, 768], P(('cache', 'mp')), may hold values from -6 to 6
- refresh_ids: int32 [4096], P(('cache', 'mp')), may hold values from 0 to 131071, as said below
- queries: bfloat16 [16384, 768], P(('cache', 'mp')), may hold values from -110 to 110
- neg_blocks: int32 [16384, 8], P(('cache', 'mp')), may hold values from 0 to 1023, all different within a row; in each aligned block of 128 rows (0 to 127, 128 to 255, ...) at most 2 rows name the same one
- positive_ids: int32 [16384], P(('cache', 'mp')), may hold values from 0 to 31
Outputs:
- new_cache: bfloat16 [131072, 768], P(('cache', 'mp'))
- loss: float32 [16384], P(('cache', 'mp'))
- query_grad: float32 [16384, 768], P(('cache', 'mp'))
The draws below stay inside these ranges and needn't reach their ends.
Inputs may be any that keep to these rules, and one draw needn't show every extreme that they name: `refresh_ids`: all ids differ. The documents of one device name at most 2 rows within any one range of 4096 rows that one index of cache holds, and in every draw one such range receives exactly 2 rows from every device. `neg_blocks`: each query lists 8 different blocks. The queries of one device list one block at most 2 times, and some block exactly that often.
All inputs are finite; a program needn't handle non-finite values.
Results may differ from the reference program's by a relative error of at most 0.0034.
Values may be sent and summed in bfloat16 or wider, within the bound.
A program may use at most 128 MiB of HBM per device.

```python
import math
import jax
import jax.numpy as jnp
import numpy as np
from jax import lax

D = 768
FF = 3072
BLOCK = 128
DLEN = 64
NEG = 8
RD = 32
QDEV = 128
ROWS_GRP = 4096
ROWS = 131072
NBLK = 1024
CAPR = 2
CAPB = 2
DOCS = 4096
TOKENS = 262144
QUERIES = 16384
N_CACHE = 32
N_MP = 4


def draw_refresh_ids(key, part):
    key_hot = jax.random.fold_in(key, 11)
    key_perm = jax.random.fold_in(key, 12)
    key_source = jax.random.fold_in(key, 13)
    hot_group = jax.random.randint(key_hot, (), 0, N_CACHE)
    tables = jax.vmap(lambda index: jax.random.permutation(jax.random.fold_in(key_perm, index), ROWS_GRP))(jnp.arange(N_CACHE))

    def one_source(source):
        key_here = jax.random.fold_in(key_source, source)
        key_pick = jax.random.fold_in(key_here, 1)
        key_order = jax.random.fold_in(key_here, 2)
        others = jax.random.permutation(key_pick, (N_CACHE - 1) * CAPR)
        other_group = others // CAPR
        other_group = other_group + (other_group >= hot_group).astype(jnp.int32)
        other_slot = other_group * CAPR + others % CAPR
        chosen = jnp.concatenate([hot_group * CAPR + jnp.arange(CAPR, dtype=jnp.int32), other_slot[:RD - CAPR].astype(jnp.int32)])
        chosen = chosen[jax.random.permutation(key_order, RD)]
        group_of = chosen // CAPR
        rank_of = chosen % CAPR
        in_group = tables[group_of, source * CAPR + rank_of]
        return group_of * ROWS_GRP + in_group
    return jax.vmap(one_source)(jnp.arange(N_CACHE * N_MP)).reshape(-1).astype(jnp.int32)


def draw_queries(key, part):
    key_rows = jax.random.fold_in(key, 21)
    rows = 2.0 * jax.random.normal(key_rows, (QUERIES, D), jnp.float32)
    return jnp.clip(rows, -8.0, 8.0).astype(jnp.bfloat16)


def touch_ends(values, own_key, smallest, largest):
    shape = values.shape
    index_at = [jax.random.randint(jax.random.fold_in(own_key, axis), (), 0, shape[axis]) for axis in range(len(shape))]
    values = values.at[tuple(index_at)].set(smallest)
    longest = shape.index(max(shape))
    index_at[longest] = (index_at[longest] + 1) % shape[longest]
    return values.at[tuple(index_at)].set(largest)


def steps_of(stream_key, extent, cuts, least, largest):
    gain = 1.0
    for position, parts in cuts:
        steps = jax.random.uniform(jax.random.fold_in(jax.random.fold_in(stream_key, 6), position), (parts,), jnp.float32, least / len(cuts), largest / len(cuts))
        gain = gain * jnp.repeat(jnp.exp(steps), extent[position] // parts).reshape((-1,) + (1,) * (len(extent) - 1 - position))
    return gain


def shared_out(own_key, own, number, rows, amount, top, reach, lean):
    order = jax.random.permutation(own_key, amount)
    heavy_load, usual = portions_of(amount, rows * top, reach, lean, True), portions_of(amount, rows * top, reach, lean, False)
    places = jnp.arange(amount)

    def named(tallies, rotation):
        used = int((tallies > 0).sum())
        fixed = max(1, used // 4)
        moved = fixed + (places - fixed + rotation * (used - fixed)) % max(1, amount - fixed)
        return jnp.zeros((amount,), jnp.int32).at[order[jnp.where(places < fixed, places, moved)]].set(jnp.asarray(tallies, jnp.int32))

    tallies = jnp.where(number % 4 == 0, named(heavy_load, number // 4), named(usual, number - number // 4 - 1))
    mixed = jax.random.permutation(jax.random.fold_in(own, 3), amount)
    donor, sink = mixed[0:amount // 2 * 2:2], mixed[1:amount // 2 * 2:2]
    margin = jnp.minimum(tallies[donor] - 1, reach - tallies[sink]) // 2
    margin = jnp.where((donor == order[0]) | (sink == order[0]) | (tallies[sink] == 0), 0, jnp.maximum(margin, 0))
    moved = jax.random.randint(jax.random.fold_in(own, 4), (amount // 2,), 0, 1 << 20) % (margin + 1)
    tallies = tallies.at[donor].add(-moved).at[sink].add(moved)
    members = jnp.searchsorted(jnp.cumsum(tallies), jnp.arange(rows * top), side="right").astype(jnp.int32)
    listing = members.reshape(top, rows).T
    listing = listing[jax.random.permutation(jax.random.fold_in(own, 1), rows)]
    rotation = jax.random.randint(jax.random.fold_in(own, 2), (rows, 1), 0, top)
    return jnp.take_along_axis(listing, (jnp.arange(top)[None, :] + rotation) % top, axis=1)


def portions_of(amount, total, limit, slope, full):
    loads = [(1 << 20) // math.isqrt(grade ** slope) + 1 for grade in range(1, amount + 1)]
    largest = limit if full else min(limit, max(-(-total // amount), total * loads[0] // sum(loads)))
    least = 1 if total - largest >= amount - 1 else 0
    counts, surplus = [largest] + [least] * (amount - 1), total - largest - least * (amount - 1)
    while surplus > 0:
        movable = [i for i in range(1, amount) if counts[i] < largest] or [i for i in range(1, amount) if counts[i] < limit]
        mass, remaining = sum([loads[i] for i in movable]), surplus
        for i in movable:
            extra = min(limit - counts[i], max(1, remaining * loads[i] // mass), surplus)
            counts[i] = counts[i] + extra
            surplus = surplus - extra
    return np.array(counts)


def bell_draw(rng, extent, deviation, most, shards=(), kind=jnp.bfloat16):
    array = jax.random.normal(rng, extent, jnp.float32) * deviation
    if len(shards) > 0:
        array = steps_of(rng, extent, shards, -0.22, 0.18) * array
    return jnp.clip(array, min=-most, max=most).astype(kind)


def setup_inputs(seed: int = 0) -> dict:
    keys = jax.random.split(jax.random.key(seed), 11)
    tokens = bell_draw(keys[0], (TOKENS, D), 1.0, 6.0, ((0, 128),))
    w_in = bell_draw(keys[1], (D, FF), D ** -0.5, 0.21875, ((1, 4),))
    w_out = bell_draw(keys[2], (FF, D), FF ** -0.5, 0.109375, ((0, 4),))
    gain_in = jnp.clip(1.0 + 0.18 * jax.random.normal(keys[3], (D,), jnp.float32), 0.1, 1.9)
    gain_out = jnp.clip(1.0 + 0.18 * jax.random.normal(keys[4], (D,), jnp.float32), 0.1, 1.9)
    stale_cache = bell_draw(keys[5], (ROWS, D), 1.0, 6.0, ((0, 128),))
    refresh_ids = draw_refresh_ids(jax.random.fold_in(keys[10], 71), 0)
    queries = draw_queries(jax.random.fold_in(keys[10], 71), 0)
    neg_blocks_keys = jax.random.split(jax.random.fold_in(keys[8], 1), QUERIES // QDEV)
    neg_blocks_turns = jax.random.permutation(jax.random.fold_in(keys[8], 3), QUERIES // QDEV)
    neg_blocks = jax.vmap(lambda own, number: shared_out(jax.random.fold_in(keys[8], 2), own, number, QDEV, NBLK, NEG, CAPB, 2))(neg_blocks_keys, neg_blocks_turns).reshape((QUERIES, NEG))
    positive_ids = touch_ends(jax.random.randint(keys[9], (QUERIES,), 0, RD), jax.random.fold_in(keys[9], 1), 0, RD - 1).astype(jnp.int32)
    return {"tokens": tokens, "w_in": w_in, "w_out": w_out, "gain_in": gain_in, "gain_out": gain_out, "stale_cache": stale_cache, "refresh_ids": refresh_ids, "queries": queries, "neg_blocks": neg_blocks, "positive_ids": positive_ids}


epsilon = 1e-06

def norm_rows(values):
    return values * lax.rsqrt(lax.optimization_barrier(jnp.mean(values * values, axis=-1, keepdims=True)) + epsilon)

def encode(token_rows, w_in, w_out, gain_in, gain_out):
    states = token_rows.astype(jnp.float32)
    normed = (norm_rows(states) * gain_in).astype(jnp.bfloat16)
    hidden = jnp.maximum(jnp.dot(normed, w_in, preferred_element_type=jnp.float32), 0.0).astype(jnp.bfloat16)
    state_sum = states + jnp.dot(hidden, w_out, preferred_element_type=jnp.float32)
    final_rows = norm_rows(state_sum) * gain_out
    pooled = lax.optimization_barrier(jnp.mean(final_rows.reshape(-1, DLEN, D), axis=1))
    return norm_rows(pooled).astype(jnp.bfloat16)

def reference(tokens, w_in, w_out, gain_in, gain_out, stale_cache, refresh_ids, queries, neg_blocks, positive_ids):
    grouped = tokens.reshape(N_CACHE * N_MP, RD * DLEN, D)
    documents = lax.map(lambda rows_here: encode(rows_here, w_in, w_out, gain_in, gain_out), grouped).reshape(DOCS, D)
    new_cache = stale_cache.at[refresh_ids].set(documents)
    block_keys = new_cache.reshape(NBLK, BLOCK, D)
    logit_scale = D ** (-0.5)
    doc_index = jnp.arange(QUERIES, dtype=jnp.int32) // QDEV * RD + positive_ids
    positive = documents[doc_index]

    def score_span(items):
        query_rows, block_ids, positive_rows = items
        chosen = block_keys[block_ids].astype(jnp.float32)
        query_f = query_rows.astype(jnp.float32)
        logits = jnp.einsum('qd,qnkd->qnk', query_f, chosen) * logit_scale
        peak = lax.optimization_barrier(jnp.max(logits, axis=-1))
        exp_terms = jnp.exp(logits - peak[..., None])
        block_total = lax.optimization_barrier(jnp.sum(exp_terms, axis=-1))
        weights = exp_terms.astype(jnp.bfloat16).astype(jnp.float32)
        mixture = jnp.einsum('qnk,qnkd->qnd', weights, chosen)
        positive_f = positive_rows.astype(jnp.float32)
        positive_logit = lax.optimization_barrier(jnp.sum(query_f * positive_f, axis=-1)) * logit_scale
        top_value = jnp.maximum(lax.optimization_barrier(jnp.max(peak, axis=-1)), positive_logit)
        block_weight = jnp.exp(peak - top_value[:, None])
        positive_weight = jnp.exp(positive_logit - top_value)
        partition = lax.optimization_barrier(jnp.sum(block_weight * block_total, axis=-1)) + positive_weight
        loss_rows = top_value + jnp.log(partition) - positive_logit
        pulled = jnp.einsum('qn,qnd->qd', block_weight, mixture) + positive_weight[:, None] * positive_f
        grad_rows = logit_scale * (pulled / partition[:, None] - positive_f)
        return (loss_rows, grad_rows)
    span_count = QUERIES // 8
    loss, query_grad = lax.map(score_span, (queries.reshape(span_count, 8, D), neg_blocks.reshape(span_count, 8, NEG), positive.reshape(span_count, 8, D)))
    return (new_cache, loss.reshape(QUERIES), query_grad.reshape(QUERIES, D))
```

```python
import jax
import jax.numpy as jnp
from jax import lax
from jax.sharding import Mesh, PartitionSpec as P

D = 768
BLOCK = 128


epsilon = 1e-06
CACHE = ("chip", "core")


def norm_rows(values):
    values = values.astype(jnp.float32)
    return values * lax.rsqrt(jnp.mean(values * values, axis=-1, keepdims=True) + epsilon)


def shards(
    tokens,
    w_in,
    w_out,
    gain_in,
    gain_out,
    stale_cache,
    refresh_ids,
    queries,
    neg_blocks,
    positive_ids,
):
    cache_count = lax.axis_size(CACHE)
    mp_count = lax.axis_size("mp")
    docs_here = refresh_ids.shape[0]
    tok_rows = tokens.shape[0]
    doc_len = tok_rows // docs_here
    width = tokens.shape[1]
    logit_scale = D ** (-0.5)
    normed = (norm_rows(tokens) * gain_in).astype(jnp.bfloat16)
    chip_count = lax.axis_size("chip")
    core_count = lax.axis_size("core")
    piece_count = chip_count * core_count
    piece_rows = w_in.shape[0] // piece_count
    piece_at = (lax.axis_index("core") * chip_count + lax.axis_index("chip")) * piece_rows
    own_piece = jnp.stack(
        [
            lax.dynamic_slice_in_dim(w_in, piece_at, piece_rows, axis=0),
            lax.dynamic_slice_in_dim(w_out, piece_at, piece_rows, axis=0),
        ]
    )
    mp_pieces = lax.all_gather(own_piece, "mp", axis=0, tiled=False)
    mp_twice = jnp.concatenate([mp_pieces, mp_pieces], axis=0)
    other_pieces = lax.dynamic_slice_in_dim(mp_twice, lax.axis_index("mp") + 1, mp_count - 1, axis=0)
    chip_pieces = lax.all_gather(other_pieces, "chip", axis=0, tiled=False)
    all_pieces = lax.all_gather(chip_pieces, "core", axis=0, tiled=False)
    all_pieces = all_pieces.reshape(piece_count, mp_count - 1, 2, piece_rows, -1)
    w_in_rest = jnp.transpose(all_pieces[:, :, 0], (0, 2, 1, 3)).reshape(w_in.shape[0], -1)
    w_out_rest = jnp.transpose(all_pieces[:, :, 1], (1, 0, 2, 3)).reshape(-1, width)
    hidden_own = jnp.maximum(
        jnp.dot(normed, w_in, preferred_element_type=jnp.float32), 0.0
    ).astype(jnp.bfloat16)
    hidden_rest = jnp.maximum(
        jnp.dot(normed, w_in_rest, preferred_element_type=jnp.float32), 0.0
    ).astype(jnp.bfloat16)
    mixed = jnp.dot(hidden_own, w_out, preferred_element_type=jnp.float32) + jnp.dot(
        hidden_rest, w_out_rest, preferred_element_type=jnp.float32
    )
    state_sum = tokens.astype(jnp.float32) + mixed
    final_rows = norm_rows(state_sum) * gain_out
    pooled = jnp.mean(final_rows.reshape(docs_here, doc_len, width), axis=1)
    embedded = norm_rows(pooled).astype(jnp.bfloat16)
    rows_own = stale_cache.shape[0]
    group_rows = rows_own * mp_count
    refresh_cap = 2 * docs_here // cache_count
    group_of = refresh_ids // group_rows
    group_hits = (group_of[:, None] == jnp.arange(cache_count, dtype=jnp.int32)[None, :]).astype(
        jnp.int32
    )
    rank_in = jnp.sum(group_hits * (jnp.cumsum(group_hits, axis=0) - 1), axis=1)
    slot_of = group_of * refresh_cap + rank_in
    filled = (
        jnp.full((cache_count * refresh_cap,), -1, jnp.int32)
        .at[slot_of]
        .set(jnp.arange(docs_here, dtype=jnp.int32))
    )
    slot_used = filled >= 0
    slot_doc = jnp.maximum(filled, 0)
    out_rows = jnp.where(slot_used[:, None], embedded[slot_doc], jnp.zeros((), jnp.bfloat16))
    out_ids = jnp.where(slot_used, refresh_ids[slot_doc], -1)
    got_rows, got_ids = (
        lax.all_to_all(out_rows, CACHE, split_axis=0, concat_axis=0, tiled=True),
        lax.all_to_all(out_ids, CACHE, split_axis=0, concat_axis=0, tiled=True),
    )
    all_rows, all_ids = (
        lax.all_gather(got_rows, "mp", axis=0, tiled=True),
        lax.all_gather(got_ids, "mp", axis=0, tiled=True),
    )
    row_base = (lax.axis_index(CACHE) * mp_count + lax.axis_index("mp")) * rows_own
    local_row = all_ids - row_base
    write_table = jnp.arange(rows_own, dtype=jnp.int32)[:, None] == local_row[None, :]
    placed = jnp.dot(
        write_table.astype(jnp.bfloat16), all_rows, preferred_element_type=jnp.float32
    ).astype(jnp.bfloat16)
    written = jnp.any(write_table, axis=1)
    fresh_cache = jnp.where(written[:, None], placed, stale_cache)
    local_blocks = rows_own // BLOCK
    device_count = cache_count * mp_count
    block_count = local_blocks * device_count
    query_count, neg_count = neg_blocks.shape
    pair_count = query_count * neg_count
    query_cap = max(2, 2 * pair_count // block_count)
    pair_blocks = neg_blocks.reshape(-1)
    pair_marks = (pair_blocks[:, None] == jnp.arange(block_count, dtype=jnp.int32)[None, :]).astype(
        jnp.int32
    )
    pair_rank = jnp.sum(pair_marks * (jnp.cumsum(pair_marks, axis=0) - 1), axis=1)
    pair_slots = pair_blocks * query_cap + pair_rank
    slot_pair = (
        jnp.full((block_count * query_cap,), -1, jnp.int32)
        .at[pair_slots]
        .set(jnp.arange(pair_count, dtype=jnp.int32))
    )
    outbound = jnp.where(
        (slot_pair >= 0)[:, None],
        queries[jnp.maximum(slot_pair, 0) // neg_count],
        jnp.zeros((), jnp.bfloat16),
    )
    arrived = lax.all_to_all(outbound, CACHE + ("mp",), split_axis=0, concat_axis=0, tiled=True)
    arrived = arrived.reshape(device_count, local_blocks, query_cap, width)
    block_keys = fresh_cache.reshape(local_blocks, BLOCK, width)
    scores = (
        jnp.einsum("snkd,nrd->snkr", arrived, block_keys, preferred_element_type=jnp.float32)
        * logit_scale
    )
    block_peak = jnp.max(scores, axis=-1)
    exp_terms = jnp.exp(scores - block_peak[..., None])
    block_total = jnp.sum(exp_terms, axis=-1)
    weights = exp_terms.astype(jnp.bfloat16)
    mixture = jnp.einsum("snkr,nrd->snkd", weights, block_keys, preferred_element_type=jnp.float32)
    back_mix, back_peak, back_total = (
        lax.all_to_all(
            mixture.reshape(-1, width), CACHE + ("mp",), split_axis=0, concat_axis=0, tiled=True
        ),
        lax.all_to_all(
            block_peak.reshape(-1), CACHE + ("mp",), split_axis=0, concat_axis=0, tiled=True
        ),
        lax.all_to_all(
            block_total.reshape(-1), CACHE + ("mp",), split_axis=0, concat_axis=0, tiled=True
        ),
    )
    pair_mix = back_mix[pair_slots].reshape(query_count, neg_count, width)
    pair_peak = back_peak[pair_slots].reshape(query_count, neg_count)
    pair_total = back_total[pair_slots].reshape(query_count, neg_count)
    pick_table = (positive_ids[:, None] == jnp.arange(docs_here, dtype=jnp.int32)[None, :]).astype(
        jnp.bfloat16
    )
    positive = jnp.dot(pick_table, embedded, preferred_element_type=jnp.float32).astype(
        jnp.bfloat16
    )
    positive_f = positive.astype(jnp.float32)
    positive_logit = jnp.sum(queries.astype(jnp.float32) * positive_f, axis=-1) * logit_scale
    top_value = jnp.maximum(jnp.max(pair_peak, axis=-1), positive_logit)
    block_weight = jnp.exp(pair_peak - top_value[:, None])
    positive_weight = jnp.exp(positive_logit - top_value)
    partition = jnp.sum(block_weight * pair_total, axis=-1) + positive_weight
    loss = top_value + jnp.log(partition) - positive_logit
    pulled = (
        jnp.einsum("qn,qnd->qd", block_weight, pair_mix) + positive_weight[:, None] * positive_f
    )
    query_grad = logit_scale * (pulled / partition[:, None] - positive_f)
    return (fresh_cache, loss, query_grad)


def solution(mesh):
    placed = (
        P(CACHE + ("mp",), None),
        P(None, "mp"),
        P("mp", None),
        P(),
        P(),
        P(CACHE + ("mp",), None),
        P(CACHE + ("mp",)),
        P(CACHE + ("mp",), None),
        P(CACHE + ("mp",), None),
        P(CACHE + ("mp",)),
    )
    core_count = 2
    split_mesh = Mesh(
        mesh.devices.reshape(mesh.shape["cache"] // core_count, core_count, mesh.shape["mp"]),
        ("chip", "core", "mp"),
    )
    return jax.shard_map(
        shards,
        mesh=split_mesh,
        in_specs=placed,
        out_specs=(P(CACHE + ("mp",), None), P(CACHE + ("mp",)), P(CACHE + ("mp",), None)),
        check_vma=False,
    )
```

```python
import jax
import jax.numpy as jnp
from jax import lax
from jax.sharding import Mesh, PartitionSpec as P

D = 768
BLOCK = 128


epsilon = 1e-06
CACHE = ("chip", "core")


def norm_rows(values):
    values = values.astype(jnp.float32)
    return values * lax.rsqrt(jnp.mean(values * values, axis=-1, keepdims=True) + epsilon)


def shards(
    tokens,
    w_in,
    w_out,
    gain_in,
    gain_out,
    stale_cache,
    refresh_ids,
    queries,
    neg_blocks,
    positive_ids,
):
    cache_count = lax.axis_size(CACHE)
    mp_count = lax.axis_size("mp")
    docs_here = refresh_ids.shape[0]
    tok_rows = tokens.shape[0]
    doc_len = tok_rows // docs_here
    width = tokens.shape[1]
    logit_scale = D ** (-0.5)
    normed = (norm_rows(tokens) * gain_in).astype(jnp.bfloat16)
    piece_count = cache_count
    piece_rows = w_out.shape[0] // piece_count
    piece_at = lax.axis_index(CACHE) * piece_rows
    own_piece = lax.dynamic_slice_in_dim(w_out, piece_at, piece_rows, axis=0)
    mp_pieces = lax.all_to_all(
        jnp.broadcast_to(own_piece[None], (mp_count,) + own_piece.shape),
        "mp",
        split_axis=0,
        concat_axis=0,
        tiled=True,
    )
    all_pieces = lax.all_to_all(
        jnp.broadcast_to(mp_pieces[None], (piece_count,) + mp_pieces.shape),
        CACHE,
        split_axis=0,
        concat_axis=0,
        tiled=True,
    )
    w_out_full = jnp.transpose(all_pieces, (1, 0, 2, 3)).reshape(-1, width)
    hidden = jnp.maximum(
        jnp.dot(
            normed,
            lax.all_gather(w_in, "mp", axis=1, tiled=True),
            preferred_element_type=jnp.float32,
        ),
        0.0,
    ).astype(jnp.bfloat16)
    mixed = jnp.dot(hidden, w_out_full, preferred_element_type=jnp.float32)
    state_sum = tokens.astype(jnp.float32) + mixed
    final_rows = norm_rows(state_sum) * gain_out
    pooled = jnp.mean(final_rows.reshape(docs_here, doc_len, width), axis=1)
    embedded = norm_rows(pooled).astype(jnp.bfloat16)
    rows_own = stale_cache.shape[0]
    group_rows = rows_own * mp_count
    refresh_cap = 2 * docs_here // cache_count
    group_of = refresh_ids // group_rows
    group_hits = (group_of[:, None] == jnp.arange(cache_count, dtype=jnp.int32)[None, :]).astype(
        jnp.int32
    )
    rank_in = jnp.sum(group_hits * (jnp.cumsum(group_hits, axis=0) - 1), axis=1)
    slot_of = group_of * refresh_cap + rank_in
    filled = (
        jnp.full((cache_count * refresh_cap,), -1, jnp.int32)
        .at[slot_of]
        .set(jnp.arange(docs_here, dtype=jnp.int32))
    )
    slot_used = filled >= 0
    slot_doc = jnp.maximum(filled, 0)
    out_rows = jnp.where(slot_used[:, None], embedded[slot_doc], jnp.zeros((), jnp.bfloat16))
    out_ids = jnp.where(slot_used, refresh_ids[slot_doc], -1)
    got_rows, got_ids = (
        lax.all_to_all(out_rows, CACHE, split_axis=0, concat_axis=0, tiled=True),
        lax.all_to_all(out_ids, CACHE, split_axis=0, concat_axis=0, tiled=True),
    )
    all_rows, all_ids = (
        lax.all_gather(got_rows, "mp", axis=0, tiled=True),
        lax.all_gather(got_ids, "mp", axis=0, tiled=True),
    )
    row_base = (lax.axis_index(CACHE) * mp_count + lax.axis_index("mp")) * rows_own
    local_row = all_ids - row_base
    write_table = jnp.arange(rows_own, dtype=jnp.int32)[:, None] == local_row[None, :]
    placed = jnp.dot(
        write_table.astype(jnp.bfloat16), all_rows, preferred_element_type=jnp.float32
    ).astype(jnp.bfloat16)
    written = jnp.any(write_table, axis=1)
    fresh_cache = jnp.where(written[:, None], placed, stale_cache)
    local_blocks = rows_own // BLOCK
    device_count = cache_count * mp_count
    block_count = local_blocks * device_count
    query_count, neg_count = neg_blocks.shape
    pair_count = query_count * neg_count
    query_cap = max(2, 2 * pair_count // block_count)
    pair_blocks = neg_blocks.reshape(-1)
    pair_marks = (pair_blocks[:, None] == jnp.arange(block_count, dtype=jnp.int32)[None, :]).astype(
        jnp.int32
    )
    pair_rank = jnp.sum(pair_marks * (jnp.cumsum(pair_marks, axis=0) - 1), axis=1)
    pair_slots = pair_blocks * query_cap + pair_rank
    slot_pair = (
        jnp.full((block_count * query_cap,), -1, jnp.int32)
        .at[pair_slots]
        .set(jnp.arange(pair_count, dtype=jnp.int32))
    )
    outbound = jnp.where(
        (slot_pair >= 0)[:, None],
        queries[jnp.maximum(slot_pair, 0) // neg_count],
        jnp.zeros((), jnp.bfloat16),
    )
    arrived = lax.all_to_all(outbound, CACHE + ("mp",), split_axis=0, concat_axis=0, tiled=True)
    arrived = arrived.reshape(device_count, local_blocks, query_cap, width)
    block_keys = fresh_cache.reshape(local_blocks, BLOCK, width)
    scores = (
        jnp.einsum("snkd,nrd->snkr", arrived, block_keys, preferred_element_type=jnp.float32)
        * logit_scale
    )
    block_peak = jnp.max(scores, axis=-1)
    exp_terms = jnp.exp(scores - block_peak[..., None])
    block_total = jnp.sum(exp_terms, axis=-1)
    weights = exp_terms.astype(jnp.bfloat16)
    mixture = jnp.einsum("snkr,nrd->snkd", weights, block_keys, preferred_element_type=jnp.float32)
    back_mix, back_peak, back_total = (
        lax.all_to_all(
            mixture.reshape(-1, width), CACHE + ("mp",), split_axis=0, concat_axis=0, tiled=True
        ),
        lax.all_to_all(
            block_peak.reshape(-1), CACHE + ("mp",), split_axis=0, concat_axis=0, tiled=True
        ),
        lax.all_to_all(
            block_total.reshape(-1), CACHE + ("mp",), split_axis=0, concat_axis=0, tiled=True
        ),
    )
    pair_mix = back_mix[pair_slots].reshape(query_count, neg_count, width)
    pair_peak = back_peak[pair_slots].reshape(query_count, neg_count)
    pair_total = back_total[pair_slots].reshape(query_count, neg_count)
    pick_table = (positive_ids[:, None] == jnp.arange(docs_here, dtype=jnp.int32)[None, :]).astype(
        jnp.bfloat16
    )
    positive = jnp.dot(pick_table, embedded, preferred_element_type=jnp.float32).astype(
        jnp.bfloat16
    )
    positive_f = positive.astype(jnp.float32)
    positive_logit = jnp.sum(queries.astype(jnp.float32) * positive_f, axis=-1) * logit_scale
    top_value = jnp.maximum(jnp.max(pair_peak, axis=-1), positive_logit)
    block_weight = jnp.exp(pair_peak - top_value[:, None])
    positive_weight = jnp.exp(positive_logit - top_value)
    partition = jnp.sum(block_weight * pair_total, axis=-1) + positive_weight
    loss = top_value + jnp.log(partition) - positive_logit
    pulled = (
        jnp.einsum("qn,qnd->qd", block_weight, pair_mix) + positive_weight[:, None] * positive_f
    )
    query_grad = logit_scale * (pulled / partition[:, None] - positive_f)
    return (fresh_cache, loss, query_grad)


def solution(mesh):
    placed = (
        P(CACHE + ("mp",), None),
        P(None, "mp"),
        P("mp", None),
        P(),
        P(),
        P(CACHE + ("mp",), None),
        P(CACHE + ("mp",)),
        P(CACHE + ("mp",), None),
        P(CACHE + ("mp",), None),
        P(CACHE + ("mp",)),
    )
    core_count = 2
    split_mesh = Mesh(
        mesh.devices.reshape(mesh.shape["cache"] // core_count, core_count, mesh.shape["mp"]),
        ("chip", "core", "mp"),
    )
    return jax.shard_map(
        shards,
        mesh=split_mesh,
        in_specs=placed,
        out_specs=(P(CACHE + ("mp",), None), P(CACHE + ("mp",)), P(CACHE + ("mp",), None)),
        check_vma=False,
    )
```

```python
import jax
import jax.numpy as jnp
from jax import lax
from jax.sharding import Mesh, PartitionSpec as P

D = 768
BLOCK = 128


epsilon = 1e-06
CACHE = ("chip", "core")


def norm_rows(values):
    values = values.astype(jnp.float32)
    return values * lax.rsqrt(jnp.mean(values * values, axis=-1, keepdims=True) + epsilon)


def bf16_part(values):
    return lax.reduce_precision(values, exponent_bits=8, mantissa_bits=7)


def split_parts(peak, total, width):
    parts = []
    for values in (peak, total):
        high = bf16_part(values)
        rest = values - high
        middle = bf16_part(rest)
        parts += [high, middle, rest - middle]
    pad = 128 - len(parts)
    stacked = jnp.stack(parts, axis=-1).astype(jnp.bfloat16)
    return jnp.pad(stacked, [(0, 0)] * (stacked.ndim - 1) + [(0, pad)])


def join_parts(parts):
    return (parts[:, 0] + parts[:, 1]) + parts[:, 2]


def shards(
    tokens,
    w_in,
    w_out,
    gain_in,
    gain_out,
    stale_cache,
    refresh_ids,
    queries,
    neg_blocks,
    positive_ids,
):
    cache_count = lax.axis_size(CACHE)
    mp_count = lax.axis_size("mp")
    docs_here = refresh_ids.shape[0]
    tok_rows = tokens.shape[0]
    doc_len = tok_rows // docs_here
    width = tokens.shape[1]
    logit_scale = D ** (-0.5)
    normed = (norm_rows(tokens) * gain_in).astype(jnp.bfloat16)
    piece_count = cache_count
    piece_rows = w_out.shape[0] // piece_count
    piece_at = lax.axis_index(CACHE) * piece_rows
    own_piece = lax.dynamic_slice_in_dim(w_out, piece_at, piece_rows, axis=0)
    mp_pieces = lax.all_to_all(
        jnp.broadcast_to(own_piece[None], (mp_count,) + own_piece.shape),
        "mp",
        split_axis=0,
        concat_axis=0,
        tiled=True,
    )
    all_pieces = lax.all_to_all(
        jnp.broadcast_to(mp_pieces[:, None], (mp_count, piece_count) + own_piece.shape),
        CACHE,
        split_axis=1,
        concat_axis=1,
        tiled=True,
    )
    w_out_full = all_pieces.reshape(-1, width)
    hidden = jnp.maximum(
        jnp.dot(
            normed,
            lax.all_gather(w_in, "mp", axis=1, tiled=True),
            preferred_element_type=jnp.float32,
        ),
        0.0,
    ).astype(jnp.bfloat16)
    hidden = lax.optimization_barrier(hidden)
    mixed = jnp.dot(hidden, w_out_full, preferred_element_type=jnp.float32)
    state_sum = tokens.astype(jnp.float32) + mixed
    final_rows = norm_rows(state_sum) * gain_out
    pooled = jnp.mean(final_rows.reshape(docs_here, doc_len, width), axis=1)
    embedded = norm_rows(pooled).astype(jnp.bfloat16)
    rows_own = stale_cache.shape[0]
    group_rows = rows_own * mp_count
    refresh_cap = 2 * docs_here // cache_count
    group_of = refresh_ids // group_rows
    group_hits = (group_of[:, None] == jnp.arange(cache_count, dtype=jnp.int32)[None, :]).astype(
        jnp.int32
    )
    rank_in = jnp.sum(group_hits * (jnp.cumsum(group_hits, axis=0) - 1), axis=1)
    slot_of = group_of * refresh_cap + rank_in
    filled = (
        jnp.full((cache_count * refresh_cap,), -1, jnp.int32)
        .at[slot_of]
        .set(jnp.arange(docs_here, dtype=jnp.int32))
    )
    slot_used = filled >= 0
    slot_doc = jnp.maximum(filled, 0)
    out_rows = jnp.where(slot_used[:, None], embedded[slot_doc], jnp.zeros((), jnp.bfloat16))
    out_ids = jnp.where(slot_used, refresh_ids[slot_doc], -1)
    got_rows, got_ids = (
        lax.all_to_all(out_rows, CACHE, split_axis=0, concat_axis=0, tiled=True),
        lax.all_to_all(out_ids, CACHE, split_axis=0, concat_axis=0, tiled=True),
    )
    all_rows, all_ids = (
        lax.all_gather(got_rows, "mp", axis=0, tiled=True),
        lax.all_gather(got_ids, "mp", axis=0, tiled=True),
    )
    row_base = (lax.axis_index(CACHE) * mp_count + lax.axis_index("mp")) * rows_own
    local_row = all_ids - row_base
    write_table = jnp.arange(rows_own, dtype=jnp.int32)[:, None] == local_row[None, :]
    placed = jnp.dot(
        write_table.astype(jnp.bfloat16), all_rows, preferred_element_type=jnp.float32
    ).astype(jnp.bfloat16)
    written = jnp.any(write_table, axis=1)
    fresh_cache = jnp.where(written[:, None], placed, stale_cache)
    local_blocks = rows_own // BLOCK
    device_count = cache_count * mp_count
    block_count = local_blocks * device_count
    query_count, neg_count = neg_blocks.shape
    pair_count = query_count * neg_count
    query_cap = max(2, 2 * pair_count // block_count)
    pair_blocks = neg_blocks.reshape(-1)
    pair_marks = (pair_blocks[:, None] == jnp.arange(block_count, dtype=jnp.int32)[None, :]).astype(
        jnp.int32
    )
    pair_rank = jnp.sum(pair_marks * (jnp.cumsum(pair_marks, axis=0) - 1), axis=1)
    pair_slots = pair_blocks * query_cap + pair_rank
    slot_pair = (
        jnp.full((block_count * query_cap,), -1, jnp.int32)
        .at[pair_slots]
        .set(jnp.arange(pair_count, dtype=jnp.int32))
    )
    outbound = jnp.where(
        (slot_pair >= 0)[:, None],
        queries[jnp.maximum(slot_pair, 0) // neg_count],
        jnp.zeros((), jnp.bfloat16),
    )
    arrived = lax.all_to_all(outbound, CACHE + ("mp",), split_axis=0, concat_axis=0, tiled=True)
    arrived = arrived.reshape(device_count, local_blocks, query_cap, width)
    block_keys = fresh_cache.reshape(local_blocks, BLOCK, width)
    scores = (
        jnp.einsum("snkd,nrd->snkr", arrived, block_keys, preferred_element_type=jnp.float32)
        * logit_scale
    )
    block_peak = jnp.max(scores, axis=-1)
    exp_terms = jnp.exp(scores - block_peak[..., None])
    block_total = jnp.sum(exp_terms, axis=-1)
    weights = exp_terms.astype(jnp.bfloat16)
    mixture = jnp.einsum("snkr,nrd->snkd", weights, block_keys, preferred_element_type=jnp.float32)
    packed = jnp.concatenate(
        [mixture.astype(jnp.bfloat16), split_parts(block_peak, block_total, width)], axis=-1
    )
    back = lax.all_to_all(
        packed.reshape(-1, packed.shape[-1]), CACHE + ("mp",), split_axis=0, concat_axis=0, tiled=True
    )
    pair_back = back[pair_slots].astype(jnp.float32)
    pair_mix = pair_back[:, :width].reshape(query_count, neg_count, width)
    pair_peak = join_parts(pair_back[:, width : width + 3]).reshape(query_count, neg_count)
    pair_total = join_parts(pair_back[:, width + 3 : width + 6]).reshape(query_count, neg_count)
    pick_table = (positive_ids[:, None] == jnp.arange(docs_here, dtype=jnp.int32)[None, :]).astype(
        jnp.bfloat16
    )
    positive = jnp.dot(pick_table, embedded, preferred_element_type=jnp.float32).astype(
        jnp.bfloat16
    )
    positive_f = positive.astype(jnp.float32)
    positive_logit = jnp.sum(queries.astype(jnp.float32) * positive_f, axis=-1) * logit_scale
    top_value = jnp.maximum(jnp.max(pair_peak, axis=-1), positive_logit)
    block_weight = jnp.exp(pair_peak - top_value[:, None])
    positive_weight = jnp.exp(positive_logit - top_value)
    partition = jnp.sum(block_weight * pair_total, axis=-1) + positive_weight
    loss = top_value + jnp.log(partition) - positive_logit
    pulled = (
        jnp.einsum("qn,qnd->qd", block_weight, pair_mix) + positive_weight[:, None] * positive_f
    )
    query_grad = logit_scale * (pulled / partition[:, None] - positive_f)
    return (fresh_cache, loss, query_grad)


def solution(mesh):
    placed = (
        P(CACHE + ("mp",), None),
        P(None, "mp"),
        P("mp", None),
        P(),
        P(),
        P(CACHE + ("mp",), None),
        P(CACHE + ("mp",)),
        P(CACHE + ("mp",), None),
        P(CACHE + ("mp",), None),
        P(CACHE + ("mp",)),
    )
    core_count = 2
    split_mesh = Mesh(
        mesh.devices.reshape(mesh.shape["cache"] // core_count, core_count, mesh.shape["mp"]),
        ("chip", "core", "mp"),
    )
    return jax.shard_map(
        shards,
        mesh=split_mesh,
        in_specs=placed,
        out_specs=(P(CACHE + ("mp",), None), P(CACHE + ("mp",)), P(CACHE + ("mp",), None)),
        check_vma=False,
    )
```

```python
import jax
import jax.numpy as jnp
from jax import lax
from jax.sharding import Mesh, PartitionSpec as P

D = 768
BLOCK = 128


epsilon = 1e-06
CACHE = ("chip", "core")
CODE_BASE = 32


def norm_rows(values):
    values = values.astype(jnp.float32)
    return values * lax.rsqrt(jnp.mean(values * values, axis=-1, keepdims=True) + epsilon)


def bf16_part(values):
    return lax.reduce_precision(values, exponent_bits=8, mantissa_bits=7)


def split_parts(peak, total, width):
    parts = []
    for values in (peak, total):
        high = bf16_part(values)
        rest = values - high
        middle = bf16_part(rest)
        parts += [high, middle, rest - middle]
    pad = 128 - len(parts)
    stacked = jnp.stack(parts, axis=-1).astype(jnp.bfloat16)
    return jnp.pad(stacked, [(0, 0)] * (stacked.ndim - 1) + [(0, pad)])


def join_parts(parts):
    return (parts[:, 0] + parts[:, 1]) + parts[:, 2]


def shards(
    tokens,
    w_in,
    w_out,
    gain_in,
    gain_out,
    stale_cache,
    refresh_ids,
    queries,
    neg_blocks,
    positive_ids,
):
    cache_count = lax.axis_size(CACHE)
    mp_count = lax.axis_size("mp")
    docs_here = refresh_ids.shape[0]
    tok_rows = tokens.shape[0]
    doc_len = tok_rows // docs_here
    width = tokens.shape[1]
    logit_scale = D ** (-0.5)
    normed = (norm_rows(tokens) * gain_in).astype(jnp.bfloat16)
    piece_count = cache_count
    piece_rows = w_out.shape[0] // piece_count
    piece_at = lax.axis_index(CACHE) * piece_rows
    mp_here = lax.axis_index("mp")
    own_piece = lax.dynamic_slice_in_dim(w_out, piece_at, piece_rows, axis=0)
    mp_pieces = lax.all_to_all(
        jnp.broadcast_to(own_piece[None], (mp_count,) + own_piece.shape),
        "mp",
        split_axis=0,
        concat_axis=0,
        tiled=True,
    )
    mp_twice = jnp.concatenate([mp_pieces, mp_pieces], axis=0)
    other_pieces = lax.dynamic_slice_in_dim(mp_twice, mp_here + 1, mp_count - 1, axis=0)
    rest_pieces = lax.all_to_all(
        jnp.broadcast_to(other_pieces[:, None], (mp_count - 1, piece_count) + own_piece.shape),
        CACHE,
        split_axis=1,
        concat_axis=1,
        tiled=True,
    )
    w_out_rest = rest_pieces.reshape(-1, width)
    w_in_full = lax.all_gather(w_in, "mp", axis=1, tiled=True)
    shard_cols = w_in.shape[1]
    w_in_rest = lax.dynamic_slice_in_dim(
        jnp.concatenate([w_in_full, w_in_full], axis=1),
        (mp_here + 1) * shard_cols,
        (mp_count - 1) * shard_cols,
        axis=1,
    )
    hidden_own = jnp.maximum(
        jnp.dot(normed, w_in, preferred_element_type=jnp.float32), 0.0
    ).astype(jnp.bfloat16)
    hidden_rest = jnp.maximum(
        jnp.dot(normed, w_in_rest, preferred_element_type=jnp.float32), 0.0
    ).astype(jnp.bfloat16)
    mixed = jnp.dot(hidden_own, w_out, preferred_element_type=jnp.float32) + jnp.dot(
        hidden_rest, w_out_rest, preferred_element_type=jnp.float32
    )
    state_sum = tokens.astype(jnp.float32) + mixed
    final_rows = norm_rows(state_sum) * gain_out
    pooled = jnp.mean(final_rows.reshape(docs_here, doc_len, width), axis=1)
    embedded = norm_rows(pooled).astype(jnp.bfloat16)
    rows_own = stale_cache.shape[0]
    device_count = cache_count * mp_count
    refresh_cap = 2 * docs_here // cache_count
    dest_of = refresh_ids // rows_own
    dest_hits = (dest_of[:, None] == jnp.arange(device_count, dtype=jnp.int32)[None, :]).astype(
        jnp.int32
    )
    rank_in = jnp.sum(dest_hits * (jnp.cumsum(dest_hits, axis=0) - 1), axis=1)
    slot_of = dest_of * refresh_cap + rank_in
    filled = (
        jnp.full((device_count * refresh_cap,), -1, jnp.int32)
        .at[slot_of]
        .set(jnp.arange(docs_here, dtype=jnp.int32))
    )
    slot_used = filled >= 0
    slot_doc = jnp.maximum(filled, 0)
    code = jnp.where(slot_used, refresh_ids[slot_doc] % rows_own + 1, 0)
    code_cols = jnp.zeros((code.shape[0], 128), jnp.float32)
    code_cols = code_cols.at[:, 0].set((code // CODE_BASE).astype(jnp.float32))
    code_cols = code_cols.at[:, 1].set((code % CODE_BASE).astype(jnp.float32))
    out_rows = jnp.concatenate(
        [
            jnp.where(slot_used[:, None], embedded[slot_doc], jnp.zeros((), jnp.bfloat16)),
            code_cols.astype(jnp.bfloat16),
        ],
        axis=1,
    )
    got = lax.all_to_all(out_rows, CACHE + ("mp",), split_axis=0, concat_axis=0, tiled=True)
    got_code = got[:, width].astype(jnp.int32) * CODE_BASE + got[:, width + 1].astype(jnp.int32)
    local_row = got_code - 1
    write_table = jnp.arange(rows_own, dtype=jnp.int32)[:, None] == local_row[None, :]
    placed = jnp.dot(
        write_table.astype(jnp.bfloat16), got[:, :width], preferred_element_type=jnp.float32
    ).astype(jnp.bfloat16)
    written = jnp.any(write_table, axis=1)
    fresh_cache = jnp.where(written[:, None], placed, stale_cache)
    local_blocks = rows_own // BLOCK
    block_count = local_blocks * device_count
    query_count, neg_count = neg_blocks.shape
    pair_count = query_count * neg_count
    query_cap = max(2, 2 * pair_count // block_count)
    pair_blocks = neg_blocks.reshape(-1)
    pair_marks = (pair_blocks[:, None] == jnp.arange(block_count, dtype=jnp.int32)[None, :]).astype(
        jnp.int32
    )
    pair_rank = jnp.sum(pair_marks * (jnp.cumsum(pair_marks, axis=0) - 1), axis=1)
    pair_slots = pair_blocks * query_cap + pair_rank
    slot_pair = (
        jnp.full((block_count * query_cap,), -1, jnp.int32)
        .at[pair_slots]
        .set(jnp.arange(pair_count, dtype=jnp.int32))
    )
    outbound = jnp.where(
        (slot_pair >= 0)[:, None],
        queries[jnp.maximum(slot_pair, 0) // neg_count],
        jnp.zeros((), jnp.bfloat16),
    )
    arrived = lax.all_to_all(outbound, CACHE + ("mp",), split_axis=0, concat_axis=0, tiled=True)
    arrived = arrived.reshape(device_count, local_blocks, query_cap, width)
    block_keys = fresh_cache.reshape(local_blocks, BLOCK, width)
    scores = (
        jnp.einsum("snkd,nrd->snkr", arrived, block_keys, preferred_element_type=jnp.float32)
        * logit_scale
    )
    block_peak = jnp.max(scores, axis=-1)
    exp_terms = jnp.exp(scores - block_peak[..., None])
    block_total = jnp.sum(exp_terms, axis=-1)
    weights = exp_terms.astype(jnp.bfloat16)
    mixture = jnp.einsum("snkr,nrd->snkd", weights, block_keys, preferred_element_type=jnp.float32)
    packed = jnp.concatenate(
        [mixture.astype(jnp.bfloat16), split_parts(block_peak, block_total, width)], axis=-1
    )
    back = lax.all_to_all(
        packed.reshape(-1, packed.shape[-1]), CACHE + ("mp",), split_axis=0, concat_axis=0, tiled=True
    )
    pair_back = back[pair_slots].astype(jnp.float32)
    pair_mix = pair_back[:, :width].reshape(query_count, neg_count, width)
    pair_peak = join_parts(pair_back[:, width : width + 3]).reshape(query_count, neg_count)
    pair_total = join_parts(pair_back[:, width + 3 : width + 6]).reshape(query_count, neg_count)
    pick_table = (positive_ids[:, None] == jnp.arange(docs_here, dtype=jnp.int32)[None, :]).astype(
        jnp.bfloat16
    )
    positive = jnp.dot(pick_table, embedded, preferred_element_type=jnp.float32).astype(
        jnp.bfloat16
    )
    positive_f = positive.astype(jnp.float32)
    positive_logit = jnp.sum(queries.astype(jnp.float32) * positive_f, axis=-1) * logit_scale
    top_value = jnp.maximum(jnp.max(pair_peak, axis=-1), positive_logit)
    block_weight = jnp.exp(pair_peak - top_value[:, None])
    positive_weight = jnp.exp(positive_logit - top_value)
    partition = jnp.sum(block_weight * pair_total, axis=-1) + positive_weight
    loss = top_value + jnp.log(partition) - positive_logit
    pulled = (
        jnp.einsum("qn,qnd->qd", block_weight, pair_mix) + positive_weight[:, None] * positive_f
    )
    query_grad = logit_scale * (pulled / partition[:, None] - positive_f)
    return (fresh_cache, loss, query_grad)


def solution(mesh):
    placed = (
        P(CACHE + ("mp",), None),
        P(None, "mp"),
        P("mp", None),
        P(),
        P(),
        P(CACHE + ("mp",), None),
        P(CACHE + ("mp",)),
        P(CACHE + ("mp",), None),
        P(CACHE + ("mp",), None),
        P(CACHE + ("mp",)),
    )
    core_count = 2
    split_mesh = Mesh(
        mesh.devices.reshape(mesh.shape["cache"] // core_count, core_count, mesh.shape["mp"]),
        ("chip", "core", "mp"),
    )
    return jax.shard_map(
        shards,
        mesh=split_mesh,
        in_specs=placed,
        out_specs=(P(CACHE + ("mp",), None), P(CACHE + ("mp",)), P(CACHE + ("mp",), None)),
        check_vma=False,
    )
```

```python
import jax
import jax.numpy as jnp
from jax import lax
from jax.sharding import Mesh, PartitionSpec as P

D = 768
BLOCK = 128


epsilon = 1e-06
CACHE = ("chip", "core")
CODE_BASE = 32


def norm_rows(values):
    values = values.astype(jnp.float32)
    return values * lax.rsqrt(jnp.mean(values * values, axis=-1, keepdims=True) + epsilon)


def bf16_part(values):
    return lax.reduce_precision(values, exponent_bits=8, mantissa_bits=7)


def split_parts(peak, total, width):
    parts = []
    for values in (peak, total):
        high = bf16_part(values)
        rest = values - high
        middle = bf16_part(rest)
        parts += [high, middle, rest - middle]
    pad = 128 - len(parts)
    stacked = jnp.stack(parts, axis=-1).astype(jnp.bfloat16)
    return jnp.pad(stacked, [(0, 0)] * (stacked.ndim - 1) + [(0, pad)])


def join_parts(parts):
    return (parts[:, 0] + parts[:, 1]) + parts[:, 2]


def shards(
    tokens,
    w_in,
    w_out,
    gain_in,
    gain_out,
    stale_cache,
    refresh_ids,
    queries,
    neg_blocks,
    positive_ids,
):
    cache_count = lax.axis_size(CACHE)
    mp_count = lax.axis_size("mp")
    docs_here = refresh_ids.shape[0]
    tok_rows = tokens.shape[0]
    doc_len = tok_rows // docs_here
    width = tokens.shape[1]
    logit_scale = D ** (-0.5)
    normed = (norm_rows(tokens) * gain_in).astype(jnp.bfloat16)
    piece_count = cache_count
    piece_rows = w_out.shape[0] // piece_count
    piece_at = lax.axis_index(CACHE) * piece_rows
    own_piece = lax.dynamic_slice_in_dim(w_out, piece_at, piece_rows, axis=0)
    device_count = cache_count * mp_count
    all_pieces = lax.all_to_all(
        jnp.broadcast_to(own_piece[None], (device_count,) + own_piece.shape),
        CACHE + ("mp",),
        split_axis=0,
        concat_axis=0,
        tiled=True,
    )
    w_out_all = all_pieces.reshape(-1, width)
    w_in_full = lax.all_gather(w_in, "mp", axis=1, tiled=True)
    w_in_all = (
        w_in_full.reshape(w_in.shape[0], mp_count, piece_count, piece_rows)
        .transpose(0, 2, 1, 3)
        .reshape(w_in.shape[0], -1)
    )
    hidden = jnp.maximum(
        jnp.dot(normed, w_in_all, preferred_element_type=jnp.float32), 0.0
    ).astype(jnp.bfloat16)
    mixed = jnp.dot(hidden, w_out_all, preferred_element_type=jnp.float32)
    state_sum = tokens.astype(jnp.float32) + mixed
    final_rows = norm_rows(state_sum) * gain_out
    pooled = jnp.mean(final_rows.reshape(docs_here, doc_len, width), axis=1)
    embedded = norm_rows(pooled).astype(jnp.bfloat16)
    rows_own = stale_cache.shape[0]
    refresh_cap = 2 * docs_here // cache_count
    dest_of = refresh_ids // rows_own
    dest_hits = (dest_of[:, None] == jnp.arange(device_count, dtype=jnp.int32)[None, :]).astype(
        jnp.int32
    )
    rank_in = jnp.sum(dest_hits * (jnp.cumsum(dest_hits, axis=0) - 1), axis=1)
    slot_of = dest_of * refresh_cap + rank_in
    filled = (
        jnp.full((device_count * refresh_cap,), -1, jnp.int32)
        .at[slot_of]
        .set(jnp.arange(docs_here, dtype=jnp.int32))
    )
    slot_used = filled >= 0
    slot_doc = jnp.maximum(filled, 0)
    code = jnp.where(slot_used, refresh_ids[slot_doc] % rows_own + 1, 0)
    code_cols = jnp.zeros((code.shape[0], 128), jnp.float32)
    code_cols = code_cols.at[:, 0].set((code // CODE_BASE).astype(jnp.float32))
    code_cols = code_cols.at[:, 1].set((code % CODE_BASE).astype(jnp.float32))
    out_rows = jnp.concatenate(
        [
            jnp.where(slot_used[:, None], embedded[slot_doc], jnp.zeros((), jnp.bfloat16)),
            code_cols.astype(jnp.bfloat16),
        ],
        axis=1,
    )
    got = lax.all_to_all(out_rows, CACHE + ("mp",), split_axis=0, concat_axis=0, tiled=True)
    got_code = got[:, width].astype(jnp.int32) * CODE_BASE + got[:, width + 1].astype(jnp.int32)
    local_row = got_code - 1
    write_table = jnp.arange(rows_own, dtype=jnp.int32)[:, None] == local_row[None, :]
    placed = jnp.dot(
        write_table.astype(jnp.bfloat16), got[:, :width], preferred_element_type=jnp.float32
    ).astype(jnp.bfloat16)
    written = jnp.any(write_table, axis=1)
    fresh_cache = jnp.where(written[:, None], placed, stale_cache)
    local_blocks = rows_own // BLOCK
    block_count = local_blocks * device_count
    query_count, neg_count = neg_blocks.shape
    pair_count = query_count * neg_count
    query_cap = max(2, 2 * pair_count // block_count)
    pair_blocks = neg_blocks.reshape(-1)
    pair_marks = (pair_blocks[:, None] == jnp.arange(block_count, dtype=jnp.int32)[None, :]).astype(
        jnp.int32
    )
    pair_rank = jnp.sum(pair_marks * (jnp.cumsum(pair_marks, axis=0) - 1), axis=1)
    pair_slots = pair_blocks * query_cap + pair_rank
    slot_pair = (
        jnp.full((block_count * query_cap,), -1, jnp.int32)
        .at[pair_slots]
        .set(jnp.arange(pair_count, dtype=jnp.int32))
    )
    outbound = jnp.where(
        (slot_pair >= 0)[:, None],
        queries[jnp.maximum(slot_pair, 0) // neg_count],
        jnp.zeros((), jnp.bfloat16),
    )
    arrived = lax.all_to_all(outbound, CACHE + ("mp",), split_axis=0, concat_axis=0, tiled=True)
    arrived = arrived.reshape(device_count, local_blocks, query_cap, width)
    block_keys = fresh_cache.reshape(local_blocks, BLOCK, width)
    scores = (
        jnp.einsum("snkd,nrd->snkr", arrived, block_keys, preferred_element_type=jnp.float32)
        * logit_scale
    )
    block_peak = jnp.max(scores, axis=-1)
    exp_terms = jnp.exp(scores - block_peak[..., None])
    block_total = jnp.sum(exp_terms, axis=-1)
    weights = exp_terms.astype(jnp.bfloat16)
    mixture = jnp.einsum("snkr,nrd->snkd", weights, block_keys, preferred_element_type=jnp.float32)
    packed = jnp.concatenate(
        [mixture.astype(jnp.bfloat16), split_parts(block_peak, block_total, width)], axis=-1
    )
    back = lax.all_to_all(
        packed.reshape(-1, packed.shape[-1]), CACHE + ("mp",), split_axis=0, concat_axis=0, tiled=True
    )
    pair_back = back[pair_slots].astype(jnp.float32)
    pair_mix = pair_back[:, :width].reshape(query_count, neg_count, width)
    pair_peak = join_parts(pair_back[:, width : width + 3]).reshape(query_count, neg_count)
    pair_total = join_parts(pair_back[:, width + 3 : width + 6]).reshape(query_count, neg_count)
    pick_table = (positive_ids[:, None] == jnp.arange(docs_here, dtype=jnp.int32)[None, :]).astype(
        jnp.bfloat16
    )
    positive = jnp.dot(pick_table, embedded, preferred_element_type=jnp.float32).astype(
        jnp.bfloat16
    )
    positive_f = positive.astype(jnp.float32)
    positive_logit = jnp.sum(queries.astype(jnp.float32) * positive_f, axis=-1) * logit_scale
    top_value = jnp.maximum(jnp.max(pair_peak, axis=-1), positive_logit)
    block_weight = jnp.exp(pair_peak - top_value[:, None])
    positive_weight = jnp.exp(positive_logit - top_value)
    partition = jnp.sum(block_weight * pair_total, axis=-1) + positive_weight
    loss = top_value + jnp.log(partition) - positive_logit
    pulled = (
        jnp.einsum("qn,qnd->qd", block_weight, pair_mix) + positive_weight[:, None] * positive_f
    )
    query_grad = logit_scale * (pulled / partition[:, None] - positive_f)
    return (fresh_cache, loss, query_grad)


def solution(mesh):
    placed = (
        P(CACHE + ("mp",), None),
        P(None, "mp"),
        P("mp", None),
        P(),
        P(),
        P(CACHE + ("mp",), None),
        P(CACHE + ("mp",)),
        P(CACHE + ("mp",), None),
        P(CACHE + ("mp",), None),
        P(CACHE + ("mp",)),
    )
    core_count = 2
    split_mesh = Mesh(
        mesh.devices.reshape(mesh.shape["cache"] // core_count, core_count, mesh.shape["mp"]),
        ("chip", "core", "mp"),
    )
    return jax.shard_map(
        shards,
        mesh=split_mesh,
        in_specs=placed,
        out_specs=(P(CACHE + ("mp",), None), P(CACHE + ("mp",)), P(CACHE + ("mp",), None)),
        check_vma=False,
    )
```

```python
import jax
import jax.numpy as jnp
from jax import lax
from jax.sharding import Mesh, PartitionSpec as P

D = 768
BLOCK = 128


epsilon = 1e-06
CACHE = ("chip", "core")
CODE_BASE = 32


def norm_rows(values):
    values = values.astype(jnp.float32)
    return values * lax.rsqrt(jnp.mean(values * values, axis=-1, keepdims=True) + epsilon)


def bf16_part(values):
    return lax.reduce_precision(values, exponent_bits=8, mantissa_bits=7)


def split_parts(peak, total, width):
    parts = []
    for values in (peak, total):
        high = bf16_part(values)
        rest = values - high
        middle = bf16_part(rest)
        parts += [high, middle, rest - middle]
    pad = 128 - len(parts)
    stacked = jnp.stack(parts, axis=-1).astype(jnp.bfloat16)
    return jnp.pad(stacked, [(0, 0)] * (stacked.ndim - 1) + [(0, pad)])


def join_parts(parts):
    return (parts[:, 0] + parts[:, 1]) + parts[:, 2]


def shards(
    tokens,
    w_in,
    w_out,
    gain_in,
    gain_out,
    stale_cache,
    refresh_ids,
    queries,
    neg_blocks,
    positive_ids,
):
    cache_count = lax.axis_size(CACHE)
    mp_count = lax.axis_size("mp")
    docs_here = refresh_ids.shape[0]
    tok_rows = tokens.shape[0]
    doc_len = tok_rows // docs_here
    width = tokens.shape[1]
    logit_scale = D ** (-0.5)
    normed = (norm_rows(tokens) * gain_in).astype(jnp.bfloat16)
    chip_count = lax.axis_size("chip")
    core_count = lax.axis_size("core")
    piece_rows = w_out.shape[0] // cache_count
    piece_at = lax.axis_index(CACHE) * piece_rows
    own_piece = jnp.stack(
        [
            lax.dynamic_slice_in_dim(w_in, piece_at, piece_rows, axis=0),
            lax.dynamic_slice_in_dim(w_out, piece_at, piece_rows, axis=0),
        ]
    )
    half_pieces = lax.all_to_all(
        jnp.broadcast_to(own_piece[None], (chip_count * mp_count,) + own_piece.shape),
        ("chip", "mp"),
        split_axis=0,
        concat_axis=0,
        tiled=True,
    )
    all_pieces = lax.all_to_all(
        jnp.broadcast_to(half_pieces[None], (core_count,) + half_pieces.shape),
        "core",
        split_axis=0,
        concat_axis=0,
        tiled=True,
    )
    all_pieces = all_pieces.reshape(core_count, chip_count, mp_count, 2, piece_rows, -1)
    w_in_full = jnp.transpose(all_pieces[:, :, :, 0], (1, 0, 3, 2, 4)).reshape(w_in.shape[0], -1)
    w_out_full = jnp.transpose(all_pieces[:, :, :, 1], (2, 1, 0, 3, 4)).reshape(-1, width)
    hidden = jnp.maximum(
        jnp.dot(normed, w_in_full, preferred_element_type=jnp.float32), 0.0
    ).astype(jnp.bfloat16)
    mixed = jnp.dot(hidden, w_out_full, preferred_element_type=jnp.float32)
    state_sum = tokens.astype(jnp.float32) + mixed
    final_rows = norm_rows(state_sum) * gain_out
    pooled = jnp.mean(final_rows.reshape(docs_here, doc_len, width), axis=1)
    embedded = norm_rows(pooled).astype(jnp.bfloat16)
    rows_own = stale_cache.shape[0]
    device_count = cache_count * mp_count
    refresh_cap = 2 * docs_here // cache_count
    dest_of = refresh_ids // rows_own
    dest_hits = (dest_of[:, None] == jnp.arange(device_count, dtype=jnp.int32)[None, :]).astype(
        jnp.int32
    )
    rank_in = jnp.sum(dest_hits * (jnp.cumsum(dest_hits, axis=0) - 1), axis=1)
    slot_of = dest_of * refresh_cap + rank_in
    filled = (
        jnp.full((device_count * refresh_cap,), -1, jnp.int32)
        .at[slot_of]
        .set(jnp.arange(docs_here, dtype=jnp.int32))
    )
    slot_used = filled >= 0
    slot_doc = jnp.maximum(filled, 0)
    code = jnp.where(slot_used, refresh_ids[slot_doc] % rows_own + 1, 0)
    code_cols = jnp.zeros((code.shape[0], 128), jnp.float32)
    code_cols = code_cols.at[:, 0].set((code // CODE_BASE).astype(jnp.float32))
    code_cols = code_cols.at[:, 1].set((code % CODE_BASE).astype(jnp.float32))
    out_rows = jnp.concatenate(
        [
            jnp.where(slot_used[:, None], embedded[slot_doc], jnp.zeros((), jnp.bfloat16)),
            code_cols.astype(jnp.bfloat16),
        ],
        axis=1,
    )
    got = lax.all_to_all(out_rows, CACHE + ("mp",), split_axis=0, concat_axis=0, tiled=True)
    got_code = got[:, width].astype(jnp.int32) * CODE_BASE + got[:, width + 1].astype(jnp.int32)
    local_row = got_code - 1
    write_table = jnp.arange(rows_own, dtype=jnp.int32)[:, None] == local_row[None, :]
    placed = jnp.dot(
        write_table.astype(jnp.bfloat16), got[:, :width], preferred_element_type=jnp.float32
    ).astype(jnp.bfloat16)
    written = jnp.any(write_table, axis=1)
    fresh_cache = jnp.where(written[:, None], placed, stale_cache)
    local_blocks = rows_own // BLOCK
    block_count = local_blocks * device_count
    query_count, neg_count = neg_blocks.shape
    pair_count = query_count * neg_count
    query_cap = max(2, 2 * pair_count // block_count)
    pair_blocks = neg_blocks.reshape(-1)
    pair_marks = (pair_blocks[:, None] == jnp.arange(block_count, dtype=jnp.int32)[None, :]).astype(
        jnp.int32
    )
    pair_rank = jnp.sum(pair_marks * (jnp.cumsum(pair_marks, axis=0) - 1), axis=1)
    pair_slots = pair_blocks * query_cap + pair_rank
    slot_pair = (
        jnp.full((block_count * query_cap,), -1, jnp.int32)
        .at[pair_slots]
        .set(jnp.arange(pair_count, dtype=jnp.int32))
    )
    outbound = jnp.where(
        (slot_pair >= 0)[:, None],
        queries[jnp.maximum(slot_pair, 0) // neg_count],
        jnp.zeros((), jnp.bfloat16),
    )
    arrived = lax.all_to_all(outbound, CACHE + ("mp",), split_axis=0, concat_axis=0, tiled=True)
    arrived = arrived.reshape(device_count, local_blocks, query_cap, width)
    block_keys = fresh_cache.reshape(local_blocks, BLOCK, width)
    scores = (
        jnp.einsum("snkd,nrd->snkr", arrived, block_keys, preferred_element_type=jnp.float32)
        * logit_scale
    )
    block_peak = jnp.max(scores, axis=-1)
    exp_terms = jnp.exp(scores - block_peak[..., None])
    block_total = jnp.sum(exp_terms, axis=-1)
    weights = exp_terms.astype(jnp.bfloat16)
    mixture = jnp.einsum("snkr,nrd->snkd", weights, block_keys, preferred_element_type=jnp.float32)
    packed = jnp.concatenate(
        [mixture.astype(jnp.bfloat16), split_parts(block_peak, block_total, width)], axis=-1
    )
    back = lax.all_to_all(
        packed.reshape(-1, packed.shape[-1]), CACHE + ("mp",), split_axis=0, concat_axis=0, tiled=True
    )
    pair_back = back[pair_slots].astype(jnp.float32)
    pair_mix = pair_back[:, :width].reshape(query_count, neg_count, width)
    pair_peak = join_parts(pair_back[:, width : width + 3]).reshape(query_count, neg_count)
    pair_total = join_parts(pair_back[:, width + 3 : width + 6]).reshape(query_count, neg_count)
    pick_table = (positive_ids[:, None] == jnp.arange(docs_here, dtype=jnp.int32)[None, :]).astype(
        jnp.bfloat16
    )
    positive = jnp.dot(pick_table, embedded, preferred_element_type=jnp.float32).astype(
        jnp.bfloat16
    )
    positive_f = positive.astype(jnp.float32)
    positive_logit = jnp.sum(queries.astype(jnp.float32) * positive_f, axis=-1) * logit_scale
    top_value = jnp.maximum(jnp.max(pair_peak, axis=-1), positive_logit)
    block_weight = jnp.exp(pair_peak - top_value[:, None])
    positive_weight = jnp.exp(positive_logit - top_value)
    partition = jnp.sum(block_weight * pair_total, axis=-1) + positive_weight
    loss = top_value + jnp.log(partition) - positive_logit
    pulled = (
        jnp.einsum("qn,qnd->qd", block_weight, pair_mix) + positive_weight[:, None] * positive_f
    )
    query_grad = logit_scale * (pulled / partition[:, None] - positive_f)
    return (fresh_cache, loss, query_grad)


def solution(mesh):
    placed = (
        P(CACHE + ("mp",), None),
        P(None, "mp"),
        P("mp", None),
        P(),
        P(),
        P(CACHE + ("mp",), None),
        P(CACHE + ("mp",)),
        P(CACHE + ("mp",), None),
        P(CACHE + ("mp",), None),
        P(CACHE + ("mp",)),
    )
    core_count = 2
    split_mesh = Mesh(
        mesh.devices.reshape(mesh.shape["cache"] // core_count, core_count, mesh.shape["mp"]),
        ("chip", "core", "mp"),
    )
    return jax.shard_map(
        shards,
        mesh=split_mesh,
        in_specs=placed,
        out_specs=(P(CACHE + ("mp",), None), P(CACHE + ("mp",)), P(CACHE + ("mp",), None)),
        check_vma=False,
    )
```

```python
import jax
import jax.numpy as jnp
from jax import lax
from jax.sharding import Mesh, PartitionSpec as P

D = 768
BLOCK = 128


epsilon = 1e-06
CACHE = ("chip", "core")
CODE_BASE = 32


def norm_rows(values):
    values = values.astype(jnp.float32)
    return values * lax.rsqrt(jnp.mean(values * values, axis=-1, keepdims=True) + epsilon)


def bf16_part(values):
    return lax.reduce_precision(values, exponent_bits=8, mantissa_bits=7)


def split_parts(peak, total, width):
    parts = []
    for values in (peak, total):
        high = bf16_part(values)
        rest = values - high
        middle = bf16_part(rest)
        parts += [high, middle, rest - middle]
    pad = 128 - len(parts)
    stacked = jnp.stack(parts, axis=-1).astype(jnp.bfloat16)
    return jnp.pad(stacked, [(0, 0)] * (stacked.ndim - 1) + [(0, pad)])


def join_parts(parts):
    return (parts[:, 0] + parts[:, 1]) + parts[:, 2]


def shards(
    tokens,
    w_in,
    w_out,
    gain_in,
    gain_out,
    stale_cache,
    refresh_ids,
    queries,
    neg_blocks,
    positive_ids,
):
    cache_count = lax.axis_size(CACHE)
    mp_count = lax.axis_size("mp")
    docs_here = refresh_ids.shape[0]
    tok_rows = tokens.shape[0]
    doc_len = tok_rows // docs_here
    width = tokens.shape[1]
    logit_scale = D ** (-0.5)
    normed = (norm_rows(tokens) * gain_in).astype(jnp.bfloat16)
    piece_count = cache_count
    piece_rows = w_out.shape[0] // piece_count
    piece_at = lax.axis_index(CACHE) * piece_rows
    mp_here = lax.axis_index("mp")
    own_piece = lax.dynamic_slice_in_dim(w_out, piece_at, piece_rows, axis=0)
    mp_pieces = lax.all_to_all(
        jnp.broadcast_to(own_piece[None], (mp_count,) + own_piece.shape),
        "mp",
        split_axis=0,
        concat_axis=0,
        tiled=True,
    )
    normed, mp_pieces = lax.optimization_barrier((normed, mp_pieces))
    mp_twice = jnp.concatenate([mp_pieces, mp_pieces], axis=0)
    other_pieces = lax.dynamic_slice_in_dim(mp_twice, mp_here + 1, mp_count - 1, axis=0)
    rest_pieces = lax.all_to_all(
        jnp.broadcast_to(other_pieces[:, None], (mp_count - 1, piece_count) + own_piece.shape),
        CACHE,
        split_axis=1,
        concat_axis=1,
        tiled=True,
    )
    w_out_rest = rest_pieces.reshape(-1, width)
    w_in_full = lax.all_gather(w_in, "mp", axis=1, tiled=True)
    shard_cols = w_in.shape[1]
    w_in_rest = lax.dynamic_slice_in_dim(
        jnp.concatenate([w_in_full, w_in_full], axis=1),
        (mp_here + 1) * shard_cols,
        (mp_count - 1) * shard_cols,
        axis=1,
    )
    hidden_own = jnp.maximum(
        jnp.dot(normed, w_in, preferred_element_type=jnp.float32), 0.0
    ).astype(jnp.bfloat16)
    hidden_rest = jnp.maximum(
        jnp.dot(normed, w_in_rest, preferred_element_type=jnp.float32), 0.0
    ).astype(jnp.bfloat16)
    mixed = jnp.dot(hidden_own, w_out, preferred_element_type=jnp.float32) + jnp.dot(
        hidden_rest, w_out_rest, preferred_element_type=jnp.float32
    )
    state_sum = tokens.astype(jnp.float32) + mixed
    final_rows = norm_rows(state_sum) * gain_out
    pooled = jnp.mean(final_rows.reshape(docs_here, doc_len, width), axis=1)
    embedded = norm_rows(pooled).astype(jnp.bfloat16)
    rows_own = stale_cache.shape[0]
    device_count = cache_count * mp_count
    refresh_cap = 2 * docs_here // cache_count
    dest_of = refresh_ids // rows_own
    dest_hits = (dest_of[:, None] == jnp.arange(device_count, dtype=jnp.int32)[None, :]).astype(
        jnp.int32
    )
    rank_in = jnp.sum(dest_hits * (jnp.cumsum(dest_hits, axis=0) - 1), axis=1)
    slot_of = dest_of * refresh_cap + rank_in
    filled = (
        jnp.full((device_count * refresh_cap,), -1, jnp.int32)
        .at[slot_of]
        .set(jnp.arange(docs_here, dtype=jnp.int32))
    )
    slot_used = filled >= 0
    slot_doc = jnp.maximum(filled, 0)
    code = jnp.where(slot_used, refresh_ids[slot_doc] % rows_own + 1, 0)
    code_cols = jnp.zeros((code.shape[0], 128), jnp.float32)
    code_cols = code_cols.at[:, 0].set((code // CODE_BASE).astype(jnp.float32))
    code_cols = code_cols.at[:, 1].set((code % CODE_BASE).astype(jnp.float32))
    out_rows = jnp.concatenate(
        [
            jnp.where(slot_used[:, None], embedded[slot_doc], jnp.zeros((), jnp.bfloat16)),
            code_cols.astype(jnp.bfloat16),
        ],
        axis=1,
    )
    got = lax.all_to_all(out_rows, CACHE + ("mp",), split_axis=0, concat_axis=0, tiled=True)
    got_code = got[:, width].astype(jnp.int32) * CODE_BASE + got[:, width + 1].astype(jnp.int32)
    local_row = got_code - 1
    write_table = jnp.arange(rows_own, dtype=jnp.int32)[:, None] == local_row[None, :]
    placed = jnp.dot(
        write_table.astype(jnp.bfloat16), got[:, :width], preferred_element_type=jnp.float32
    ).astype(jnp.bfloat16)
    written = jnp.any(write_table, axis=1)
    fresh_cache = jnp.where(written[:, None], placed, stale_cache)
    local_blocks = rows_own // BLOCK
    block_count = local_blocks * device_count
    query_count, neg_count = neg_blocks.shape
    pair_count = query_count * neg_count
    query_cap = max(2, 2 * pair_count // block_count)
    pair_blocks = neg_blocks.reshape(-1)
    pair_marks = (pair_blocks[:, None] == jnp.arange(block_count, dtype=jnp.int32)[None, :]).astype(
        jnp.int32
    )
    pair_rank = jnp.sum(pair_marks * (jnp.cumsum(pair_marks, axis=0) - 1), axis=1)
    pair_slots = pair_blocks * query_cap + pair_rank
    slot_pair = (
        jnp.full((block_count * query_cap,), -1, jnp.int32)
        .at[pair_slots]
        .set(jnp.arange(pair_count, dtype=jnp.int32))
    )
    outbound = jnp.where(
        (slot_pair >= 0)[:, None],
        queries[jnp.maximum(slot_pair, 0) // neg_count],
        jnp.zeros((), jnp.bfloat16),
    )
    arrived = lax.all_to_all(outbound, CACHE + ("mp",), split_axis=0, concat_axis=0, tiled=True)
    arrived = arrived.reshape(device_count, local_blocks, query_cap, width)
    block_keys = fresh_cache.reshape(local_blocks, BLOCK, width)
    scores = (
        jnp.einsum("snkd,nrd->snkr", arrived, block_keys, preferred_element_type=jnp.float32)
        * logit_scale
    )
    block_peak = jnp.max(scores, axis=-1)
    exp_terms = jnp.exp(scores - block_peak[..., None])
    block_total = jnp.sum(exp_terms, axis=-1)
    weights = exp_terms.astype(jnp.bfloat16)
    mixture = jnp.einsum("snkr,nrd->snkd", weights, block_keys, preferred_element_type=jnp.float32)
    packed = jnp.concatenate(
        [mixture.astype(jnp.bfloat16), split_parts(block_peak, block_total, width)], axis=-1
    )
    back = lax.all_to_all(
        packed.reshape(-1, packed.shape[-1]), CACHE + ("mp",), split_axis=0, concat_axis=0, tiled=True
    )
    pair_back = back[pair_slots].astype(jnp.float32)
    pair_mix = pair_back[:, :width].reshape(query_count, neg_count, width)
    pair_peak = join_parts(pair_back[:, width : width + 3]).reshape(query_count, neg_count)
    pair_total = join_parts(pair_back[:, width + 3 : width + 6]).reshape(query_count, neg_count)
    pick_table = (positive_ids[:, None] == jnp.arange(docs_here, dtype=jnp.int32)[None, :]).astype(
        jnp.bfloat16
    )
    positive = jnp.dot(pick_table, embedded, preferred_element_type=jnp.float32).astype(
        jnp.bfloat16
    )
    positive_f = positive.astype(jnp.float32)
    positive_logit = jnp.sum(queries.astype(jnp.float32) * positive_f, axis=-1) * logit_scale
    top_value = jnp.maximum(jnp.max(pair_peak, axis=-1), positive_logit)
    block_weight = jnp.exp(pair_peak - top_value[:, None])
    positive_weight = jnp.exp(positive_logit - top_value)
    partition = jnp.sum(block_weight * pair_total, axis=-1) + positive_weight
    loss = top_value + jnp.log(partition) - positive_logit
    pulled = (
        jnp.einsum("qn,qnd->qd", block_weight, pair_mix) + positive_weight[:, None] * positive_f
    )
    query_grad = logit_scale * (pulled / partition[:, None] - positive_f)
    return (fresh_cache, loss, query_grad)


def solution(mesh):
    placed = (
        P(CACHE + ("mp",), None),
        P(None, "mp"),
        P("mp", None),
        P(),
        P(),
        P(CACHE + ("mp",), None),
        P(CACHE + ("mp",)),
        P(CACHE + ("mp",), None),
        P(CACHE + ("mp",), None),
        P(CACHE + ("mp",)),
    )
    core_count = 2
    split_mesh = Mesh(
        mesh.devices.reshape(mesh.shape["cache"] // core_count, core_count, mesh.shape["mp"]),
        ("chip", "core", "mp"),
    )
    return jax.shard_map(
        shards,
        mesh=split_mesh,
        in_specs=placed,
        out_specs=(P(CACHE + ("mp",), None), P(CACHE + ("mp",)), P(CACHE + ("mp",), None)),
        check_vma=False,
    )
```

```python
import jax
import jax.numpy as jnp
from jax import lax
from jax.sharding import Mesh, PartitionSpec as P

D = 768
BLOCK = 128


epsilon = 1e-06
CACHE = ("chip", "core")
CODE_BASE = 32


def norm_rows(values):
    values = values.astype(jnp.float32)
    return values * lax.rsqrt(jnp.mean(values * values, axis=-1, keepdims=True) + epsilon)


def bf16_part(values):
    return lax.reduce_precision(values, exponent_bits=8, mantissa_bits=7)


def split_parts(peak, total, width):
    parts = []
    for values in (peak, total):
        high = bf16_part(values)
        rest = values - high
        middle = bf16_part(rest)
        parts += [high, middle, rest - middle]
    pad = 128 - len(parts)
    stacked = jnp.stack(parts, axis=-1).astype(jnp.bfloat16)
    return jnp.pad(stacked, [(0, 0)] * (stacked.ndim - 1) + [(0, pad)])


def join_parts(parts):
    return (parts[:, 0] + parts[:, 1]) + parts[:, 2]


def shards(
    tokens,
    w_in,
    w_out,
    gain_in,
    gain_out,
    stale_cache,
    refresh_ids,
    queries,
    neg_blocks,
    positive_ids,
):
    cache_count = lax.axis_size(CACHE)
    mp_count = lax.axis_size("mp")
    docs_here = refresh_ids.shape[0]
    tok_rows = tokens.shape[0]
    doc_len = tok_rows // docs_here
    width = tokens.shape[1]
    logit_scale = D ** (-0.5)
    normed = (norm_rows(tokens) * gain_in).astype(jnp.bfloat16)
    piece_count = cache_count
    piece_rows = w_out.shape[0] // piece_count
    piece_at = lax.axis_index(CACHE) * piece_rows
    mp_here = lax.axis_index("mp")
    own_piece = lax.dynamic_slice_in_dim(w_out, piece_at, piece_rows, axis=0)
    mp_pieces = lax.all_to_all(
        jnp.broadcast_to(own_piece[None], (mp_count,) + own_piece.shape),
        "mp",
        split_axis=0,
        concat_axis=0,
        tiled=True,
    )
    normed, mp_pieces = lax.optimization_barrier((normed, mp_pieces))
    mp_twice = jnp.concatenate([mp_pieces, mp_pieces], axis=0)
    other_pieces = lax.dynamic_slice_in_dim(mp_twice, mp_here + 1, mp_count - 1, axis=0)
    rest_pieces = lax.all_to_all(
        jnp.broadcast_to(other_pieces[:, None], (mp_count - 1, piece_count) + own_piece.shape),
        CACHE,
        split_axis=1,
        concat_axis=1,
        tiled=True,
    )
    w_out_rest = rest_pieces.reshape(-1, width)
    w_in_full = lax.all_gather(w_in, "mp", axis=1, tiled=True)
    shard_cols = w_in.shape[1]
    w_in_rest = lax.dynamic_slice_in_dim(
        jnp.concatenate([w_in_full, w_in_full], axis=1),
        (mp_here + 1) * shard_cols,
        (mp_count - 1) * shard_cols,
        axis=1,
    )
    hidden_own = jnp.maximum(
        jnp.dot(normed, w_in, preferred_element_type=jnp.float32), 0.0
    ).astype(jnp.bfloat16)
    hidden_rest = jnp.maximum(
        jnp.dot(normed, w_in_rest, preferred_element_type=jnp.float32), 0.0
    ).astype(jnp.bfloat16)
    mixed = jnp.dot(hidden_own, w_out, preferred_element_type=jnp.float32) + jnp.dot(
        hidden_rest, w_out_rest, preferred_element_type=jnp.float32
    )
    state_sum = tokens.astype(jnp.float32) + mixed
    final_rows = norm_rows(state_sum) * gain_out
    pooled = jnp.mean(final_rows.reshape(docs_here, doc_len, width), axis=1)
    embedded = norm_rows(pooled).astype(jnp.bfloat16)
    rows_own = stale_cache.shape[0]
    device_count = cache_count * mp_count
    refresh_cap = 2 * docs_here // cache_count
    dest_of = refresh_ids // rows_own
    dest_hits = (dest_of[:, None] == jnp.arange(device_count, dtype=jnp.int32)[None, :]).astype(
        jnp.int32
    )
    rank_in = jnp.sum(dest_hits * (jnp.cumsum(dest_hits, axis=0) - 1), axis=1)
    slot_of = dest_of * refresh_cap + rank_in
    slot_match = slot_of[:, None] == jnp.arange(device_count * refresh_cap, dtype=jnp.int32)[None, :]
    code = jnp.sum(
        jnp.where(slot_match, (refresh_ids % rows_own + 1)[:, None], 0), axis=0
    )
    code_cols = jnp.zeros((code.shape[0], 128), jnp.float32)
    code_cols = code_cols.at[:, 0].set((code // CODE_BASE).astype(jnp.float32))
    code_cols = code_cols.at[:, 1].set((code % CODE_BASE).astype(jnp.float32))
    slot_rows = jnp.dot(
        slot_match.T.astype(jnp.bfloat16), embedded, preferred_element_type=jnp.float32
    ).astype(jnp.bfloat16)
    out_rows = jnp.concatenate([slot_rows, code_cols.astype(jnp.bfloat16)], axis=1)
    got = lax.all_to_all(out_rows, CACHE + ("mp",), split_axis=0, concat_axis=0, tiled=True)
    got_code = got[:, width].astype(jnp.int32) * CODE_BASE + got[:, width + 1].astype(jnp.int32)
    local_row = got_code - 1
    write_table = jnp.arange(rows_own, dtype=jnp.int32)[:, None] == local_row[None, :]
    placed = jnp.dot(
        write_table.astype(jnp.bfloat16), got[:, :width], preferred_element_type=jnp.float32
    ).astype(jnp.bfloat16)
    written = jnp.any(write_table, axis=1)
    fresh_cache = jnp.where(written[:, None], placed, stale_cache)
    local_blocks = rows_own // BLOCK
    block_count = local_blocks * device_count
    query_count, neg_count = neg_blocks.shape
    pair_count = query_count * neg_count
    query_cap = max(2, 2 * pair_count // block_count)
    pair_blocks = neg_blocks.reshape(-1)
    pair_marks = (pair_blocks[:, None] == jnp.arange(block_count, dtype=jnp.int32)[None, :]).astype(
        jnp.int32
    )
    pair_rank = jnp.sum(pair_marks * (jnp.cumsum(pair_marks, axis=0) - 1), axis=1)
    pair_slots = pair_blocks * query_cap + pair_rank
    slot_pair = (
        jnp.full((block_count * query_cap,), -1, jnp.int32)
        .at[pair_slots]
        .set(jnp.arange(pair_count, dtype=jnp.int32))
    )
    outbound = jnp.where(
        (slot_pair >= 0)[:, None],
        queries[jnp.maximum(slot_pair, 0) // neg_count],
        jnp.zeros((), jnp.bfloat16),
    )
    arrived = lax.all_to_all(outbound, CACHE + ("mp",), split_axis=0, concat_axis=0, tiled=True)
    arrived = arrived.reshape(device_count, local_blocks, query_cap, width)
    block_keys = fresh_cache.reshape(local_blocks, BLOCK, width)
    scores = (
        jnp.einsum("snkd,nrd->snkr", arrived, block_keys, preferred_element_type=jnp.float32)
        * logit_scale
    )
    block_peak = jnp.max(scores, axis=-1)
    exp_terms = jnp.exp(scores - block_peak[..., None])
    block_total = jnp.sum(exp_terms, axis=-1)
    weights = exp_terms.astype(jnp.bfloat16)
    mixture = jnp.einsum("snkr,nrd->snkd", weights, block_keys, preferred_element_type=jnp.float32)
    packed = jnp.concatenate(
        [mixture.astype(jnp.bfloat16), split_parts(block_peak, block_total, width)], axis=-1
    )
    back = lax.all_to_all(
        packed.reshape(-1, packed.shape[-1]), CACHE + ("mp",), split_axis=0, concat_axis=0, tiled=True
    )
    pair_back = back[pair_slots].astype(jnp.float32)
    pair_mix = pair_back[:, :width].reshape(query_count, neg_count, width)
    pair_peak = join_parts(pair_back[:, width : width + 3]).reshape(query_count, neg_count)
    pair_total = join_parts(pair_back[:, width + 3 : width + 6]).reshape(query_count, neg_count)
    pick_table = (positive_ids[:, None] == jnp.arange(docs_here, dtype=jnp.int32)[None, :]).astype(
        jnp.bfloat16
    )
    positive = jnp.dot(pick_table, embedded, preferred_element_type=jnp.float32).astype(
        jnp.bfloat16
    )
    positive_f = positive.astype(jnp.float32)
    positive_logit = jnp.sum(queries.astype(jnp.float32) * positive_f, axis=-1) * logit_scale
    top_value = jnp.maximum(jnp.max(pair_peak, axis=-1), positive_logit)
    block_weight = jnp.exp(pair_peak - top_value[:, None])
    positive_weight = jnp.exp(positive_logit - top_value)
    partition = jnp.sum(block_weight * pair_total, axis=-1) + positive_weight
    loss = top_value + jnp.log(partition) - positive_logit
    pulled = (
        jnp.einsum("qn,qnd->qd", block_weight, pair_mix) + positive_weight[:, None] * positive_f
    )
    query_grad = logit_scale * (pulled / partition[:, None] - positive_f)
    return (fresh_cache, loss, query_grad)


def solution(mesh):
    placed = (
        P(CACHE + ("mp",), None),
        P(None, "mp"),
        P("mp", None),
        P(),
        P(),
        P(CACHE + ("mp",), None),
        P(CACHE + ("mp",)),
        P(CACHE + ("mp",), None),
        P(CACHE + ("mp",), None),
        P(CACHE + ("mp",)),
    )
    core_count = 2
    split_mesh = Mesh(
        mesh.devices.reshape(mesh.shape["cache"] // core_count, core_count, mesh.shape["mp"]),
        ("chip", "core", "mp"),
    )
    return jax.shard_map(
        shards,
        mesh=split_mesh,
        in_specs=placed,
        out_specs=(P(CACHE + ("mp",), None), P(CACHE + ("mp",)), P(CACHE + ("mp",), None)),
        check_vma=False,
    )
```

```python
import jax
import jax.numpy as jnp
from jax import lax
from jax.sharding import Mesh, PartitionSpec as P

D = 768
BLOCK = 128


epsilon = 1e-06
CACHE = ("chip", "core")
CODE_BASE = 32


def norm_rows(values):
    values = values.astype(jnp.float32)
    return values * lax.rsqrt(jnp.mean(values * values, axis=-1, keepdims=True) + epsilon)


def bf16_part(values):
    return lax.reduce_precision(values, exponent_bits=8, mantissa_bits=7)


def split_parts(peak, total, width):
    parts = []
    for values in (peak, total):
        high = bf16_part(values)
        rest = values - high
        middle = bf16_part(rest)
        parts += [high, middle, rest - middle]
    pad = 128 - len(parts)
    stacked = jnp.stack(parts, axis=-1).astype(jnp.bfloat16)
    return jnp.pad(stacked, [(0, 0)] * (stacked.ndim - 1) + [(0, pad)])


def join_parts(parts):
    return (parts[:, 0] + parts[:, 1]) + parts[:, 2]


def shards(
    tokens,
    w_in,
    w_out,
    gain_in,
    gain_out,
    stale_cache,
    refresh_ids,
    queries,
    neg_blocks,
    positive_ids,
):
    cache_count = lax.axis_size(CACHE)
    mp_count = lax.axis_size("mp")
    docs_here = refresh_ids.shape[0]
    tok_rows = tokens.shape[0]
    doc_len = tok_rows // docs_here
    width = tokens.shape[1]
    logit_scale = D ** (-0.5)
    normed = (norm_rows(tokens) * gain_in).astype(jnp.bfloat16)
    piece_count = cache_count
    piece_rows = w_out.shape[0] // piece_count
    piece_at = lax.axis_index(CACHE) * piece_rows
    mp_here = lax.axis_index("mp")
    own_piece = lax.dynamic_slice_in_dim(w_out, piece_at, piece_rows, axis=0)
    mp_pieces = lax.all_to_all(
        jnp.broadcast_to(own_piece[None], (mp_count,) + own_piece.shape),
        "mp",
        split_axis=0,
        concat_axis=0,
        tiled=True,
    )
    normed, mp_pieces = lax.optimization_barrier((normed, mp_pieces))
    mp_twice = jnp.concatenate([mp_pieces, mp_pieces], axis=0)
    other_pieces = lax.dynamic_slice_in_dim(mp_twice, mp_here + 1, mp_count - 1, axis=0)
    rest_pieces = lax.all_to_all(
        jnp.broadcast_to(other_pieces[:, None], (mp_count - 1, piece_count) + own_piece.shape),
        CACHE,
        split_axis=1,
        concat_axis=1,
        tiled=True,
    )
    w_out_rest = rest_pieces.reshape(-1, width)
    w_in_full = lax.all_gather(w_in, "mp", axis=1, tiled=True)
    shard_cols = w_in.shape[1]
    w_in_rest = lax.dynamic_slice_in_dim(
        jnp.concatenate([w_in_full, w_in_full], axis=1),
        (mp_here + 1) * shard_cols,
        (mp_count - 1) * shard_cols,
        axis=1,
    )
    hidden_own = jnp.maximum(
        jnp.dot(normed, w_in, preferred_element_type=jnp.float32), 0.0
    ).astype(jnp.bfloat16)
    hidden_rest = jnp.maximum(
        jnp.dot(normed, w_in_rest, preferred_element_type=jnp.float32), 0.0
    ).astype(jnp.bfloat16)
    mixed = jnp.dot(hidden_own, w_out, preferred_element_type=jnp.float32) + jnp.dot(
        hidden_rest, w_out_rest, preferred_element_type=jnp.float32
    )
    state_sum = tokens.astype(jnp.float32) + mixed
    final_rows = norm_rows(state_sum) * gain_out
    pooled = jnp.mean(final_rows.reshape(docs_here, doc_len, width), axis=1)
    embedded = norm_rows(pooled).astype(jnp.bfloat16)
    rows_own = stale_cache.shape[0]
    device_count = cache_count * mp_count
    refresh_cap = 2 * docs_here // cache_count
    dest_of = refresh_ids // rows_own
    dest_hits = (dest_of[:, None] == jnp.arange(device_count, dtype=jnp.int32)[None, :]).astype(
        jnp.int32
    )
    rank_in = jnp.sum(dest_hits * (jnp.cumsum(dest_hits, axis=0) - 1), axis=1)
    slot_of = dest_of * refresh_cap + rank_in
    slot_match = slot_of[:, None] == jnp.arange(device_count * refresh_cap, dtype=jnp.int32)[None, :]
    code = jnp.sum(
        jnp.where(slot_match, (refresh_ids % rows_own + 1)[:, None], 0), axis=0
    )
    code_cols = jnp.zeros((code.shape[0], 128), jnp.float32)
    code_cols = code_cols.at[:, 0].set((code // CODE_BASE).astype(jnp.float32))
    code_cols = code_cols.at[:, 1].set((code % CODE_BASE).astype(jnp.float32))
    slot_rows = jnp.dot(
        slot_match.T.astype(jnp.bfloat16), embedded, preferred_element_type=jnp.float32
    ).astype(jnp.bfloat16)
    out_rows = jnp.concatenate([slot_rows, code_cols.astype(jnp.bfloat16)], axis=1)
    got = lax.all_to_all(out_rows, CACHE + ("mp",), split_axis=0, concat_axis=0, tiled=True)
    got_code = got[:, width].astype(jnp.int32) * CODE_BASE + got[:, width + 1].astype(jnp.int32)
    local_row = got_code - 1
    write_table = jnp.arange(rows_own, dtype=jnp.int32)[:, None] == local_row[None, :]
    placed = jnp.dot(
        write_table.astype(jnp.bfloat16), got[:, :width], preferred_element_type=jnp.float32
    ).astype(jnp.bfloat16)
    written = jnp.any(write_table, axis=1)
    fresh_cache = jnp.where(written[:, None], placed, stale_cache)
    local_blocks = rows_own // BLOCK
    block_count = local_blocks * device_count
    query_count, neg_count = neg_blocks.shape
    pair_count = query_count * neg_count
    query_cap = max(2, 2 * pair_count // block_count)
    pair_blocks = neg_blocks.reshape(-1)
    pair_marks = (pair_blocks[:, None] == jnp.arange(block_count, dtype=jnp.int32)[None, :]).astype(
        jnp.int32
    )
    pair_rank = jnp.sum(pair_marks * (jnp.cumsum(pair_marks, axis=0) - 1), axis=1)
    pair_slots = pair_blocks * query_cap + pair_rank
    pair_match = pair_slots[:, None] == jnp.arange(block_count * query_cap, dtype=jnp.int32)[None, :]
    slot_query = jnp.any(pair_match.reshape(query_count, neg_count, -1), axis=1)
    outbound = jnp.dot(
        slot_query.T.astype(jnp.bfloat16), queries, preferred_element_type=jnp.float32
    ).astype(jnp.bfloat16)
    arrived = lax.all_to_all(outbound, CACHE + ("mp",), split_axis=0, concat_axis=0, tiled=True)
    arrived = arrived.reshape(device_count, local_blocks, query_cap, width)
    block_keys = fresh_cache.reshape(local_blocks, BLOCK, width)
    scores = (
        jnp.einsum("snkd,nrd->snkr", arrived, block_keys, preferred_element_type=jnp.float32)
        * logit_scale
    )
    block_peak = jnp.max(scores, axis=-1)
    exp_terms = jnp.exp(scores - block_peak[..., None])
    block_total = jnp.sum(exp_terms, axis=-1)
    weights = exp_terms.astype(jnp.bfloat16)
    mixture = jnp.einsum("snkr,nrd->snkd", weights, block_keys, preferred_element_type=jnp.float32)
    packed = jnp.concatenate(
        [mixture.astype(jnp.bfloat16), split_parts(block_peak, block_total, width)], axis=-1
    )
    back = lax.all_to_all(
        packed.reshape(-1, packed.shape[-1]), CACHE + ("mp",), split_axis=0, concat_axis=0, tiled=True
    )
    pair_back = jnp.dot(
        pair_match.astype(jnp.bfloat16), back, preferred_element_type=jnp.float32
    )
    pair_mix = pair_back[:, :width].reshape(query_count, neg_count, width)
    pair_peak = join_parts(pair_back[:, width : width + 3]).reshape(query_count, neg_count)
    pair_total = join_parts(pair_back[:, width + 3 : width + 6]).reshape(query_count, neg_count)
    pick_table = (positive_ids[:, None] == jnp.arange(docs_here, dtype=jnp.int32)[None, :]).astype(
        jnp.bfloat16
    )
    positive = jnp.dot(pick_table, embedded, preferred_element_type=jnp.float32).astype(
        jnp.bfloat16
    )
    positive_f = positive.astype(jnp.float32)
    positive_logit = jnp.sum(queries.astype(jnp.float32) * positive_f, axis=-1) * logit_scale
    top_value = jnp.maximum(jnp.max(pair_peak, axis=-1), positive_logit)
    block_weight = jnp.exp(pair_peak - top_value[:, None])
    positive_weight = jnp.exp(positive_logit - top_value)
    partition = jnp.sum(block_weight * pair_total, axis=-1) + positive_weight
    loss = top_value + jnp.log(partition) - positive_logit
    pulled = (
        jnp.einsum("qn,qnd->qd", block_weight, pair_mix) + positive_weight[:, None] * positive_f
    )
    query_grad = logit_scale * (pulled / partition[:, None] - positive_f)
    return (fresh_cache, loss, query_grad)


def solution(mesh):
    placed = (
        P(CACHE + ("mp",), None),
        P(None, "mp"),
        P("mp", None),
        P(),
        P(),
        P(CACHE + ("mp",), None),
        P(CACHE + ("mp",)),
        P(CACHE + ("mp",), None),
        P(CACHE + ("mp",), None),
        P(CACHE + ("mp",)),
    )
    core_count = 2
    split_mesh = Mesh(
        mesh.devices.reshape(mesh.shape["cache"] // core_count, core_count, mesh.shape["mp"]),
        ("chip", "core", "mp"),
    )
    return jax.shard_map(
        shards,
        mesh=split_mesh,
        in_specs=placed,
        out_specs=(P(CACHE + ("mp",), None), P(CACHE + ("mp",)), P(CACHE + ("mp",), None)),
        check_vma=False,
    )
```

```python
import jax
import jax.numpy as jnp
from jax import lax
from jax.sharding import Mesh, PartitionSpec as P

D = 768
BLOCK = 128


epsilon = 1e-06
CACHE = ("chip", "core")
CODE_BASE = 32


def norm_rows(values):
    values = values.astype(jnp.float32)
    return values * lax.rsqrt(jnp.mean(values * values, axis=-1, keepdims=True) + epsilon)


def bf16_part(values):
    return lax.reduce_precision(values, exponent_bits=8, mantissa_bits=7)


def split_parts(peak, total, width):
    parts = []
    for values in (peak, total):
        high = bf16_part(values)
        rest = values - high
        middle = bf16_part(rest)
        parts += [high, middle, rest - middle]
    pad = 128 - len(parts)
    stacked = jnp.stack(parts, axis=-1).astype(jnp.bfloat16)
    return jnp.pad(stacked, [(0, 0)] * (stacked.ndim - 1) + [(0, pad)])


def join_parts(parts):
    return (parts[:, 0] + parts[:, 1]) + parts[:, 2]


def shards(
    tokens,
    w_in,
    w_out,
    gain_in,
    gain_out,
    stale_cache,
    refresh_ids,
    queries,
    neg_blocks,
    positive_ids,
):
    cache_count = lax.axis_size(CACHE)
    mp_count = lax.axis_size("mp")
    docs_here = refresh_ids.shape[0]
    tok_rows = tokens.shape[0]
    doc_len = tok_rows // docs_here
    width = tokens.shape[1]
    logit_scale = D ** (-0.5)
    normed = (norm_rows(tokens) * gain_in).astype(jnp.bfloat16)
    piece_count = cache_count
    piece_rows = w_out.shape[0] // piece_count
    piece_at = lax.axis_index(CACHE) * piece_rows
    mp_here = lax.axis_index("mp")
    own_piece = lax.dynamic_slice_in_dim(w_out, piece_at, piece_rows, axis=0)
    mp_pieces = lax.all_to_all(
        jnp.broadcast_to(own_piece[None], (mp_count,) + own_piece.shape),
        "mp",
        split_axis=0,
        concat_axis=0,
        tiled=True,
    )
    normed, mp_pieces = lax.optimization_barrier((normed, mp_pieces))
    mp_twice = jnp.concatenate([mp_pieces, mp_pieces], axis=0)
    other_pieces = lax.dynamic_slice_in_dim(mp_twice, mp_here + 1, mp_count - 1, axis=0)
    rest_pieces = lax.all_to_all(
        jnp.broadcast_to(other_pieces[None], (piece_count, mp_count - 1) + own_piece.shape),
        CACHE,
        split_axis=0,
        concat_axis=0,
        tiled=True,
    )
    w_out_rest = rest_pieces.reshape(-1, width)
    w_in_full = lax.all_gather(w_in, "mp", axis=1, tiled=True)
    shard_cols = w_in.shape[1]
    w_in_rest = lax.dynamic_slice_in_dim(
        jnp.concatenate([w_in_full, w_in_full], axis=1),
        (mp_here + 1) * shard_cols,
        (mp_count - 1) * shard_cols,
        axis=1,
    )
    w_in_rest = (
        w_in_rest.reshape(w_in.shape[0], mp_count - 1, piece_count, piece_rows)
        .transpose(0, 2, 1, 3)
        .reshape(w_in.shape[0], -1)
    )
    hidden_own = jnp.maximum(
        jnp.dot(normed, w_in, preferred_element_type=jnp.float32), 0.0
    ).astype(jnp.bfloat16)
    hidden_rest = jnp.maximum(
        jnp.dot(normed, w_in_rest, preferred_element_type=jnp.float32), 0.0
    ).astype(jnp.bfloat16)
    mixed = jnp.dot(hidden_own, w_out, preferred_element_type=jnp.float32) + jnp.dot(
        hidden_rest, w_out_rest, preferred_element_type=jnp.float32
    )
    state_sum = tokens.astype(jnp.float32) + mixed
    final_rows = norm_rows(state_sum) * gain_out
    pooled = jnp.mean(final_rows.reshape(docs_here, doc_len, width), axis=1)
    embedded = norm_rows(pooled).astype(jnp.bfloat16)
    rows_own = stale_cache.shape[0]
    device_count = cache_count * mp_count
    refresh_cap = 2 * docs_here // cache_count
    dest_of = refresh_ids // rows_own
    dest_hits = (dest_of[:, None] == jnp.arange(device_count, dtype=jnp.int32)[None, :]).astype(
        jnp.int32
    )
    rank_in = jnp.sum(dest_hits * (jnp.cumsum(dest_hits, axis=0) - 1), axis=1)
    slot_of = dest_of * refresh_cap + rank_in
    slot_match = slot_of[:, None] == jnp.arange(device_count * refresh_cap, dtype=jnp.int32)[None, :]
    code = jnp.sum(
        jnp.where(slot_match, (refresh_ids % rows_own + 1)[:, None], 0), axis=0
    )
    code_cols = jnp.zeros((code.shape[0], 128), jnp.float32)
    code_cols = code_cols.at[:, 0].set((code // CODE_BASE).astype(jnp.float32))
    code_cols = code_cols.at[:, 1].set((code % CODE_BASE).astype(jnp.float32))
    slot_rows = jnp.dot(
        slot_match.T.astype(jnp.bfloat16), embedded, preferred_element_type=jnp.float32
    ).astype(jnp.bfloat16)
    out_rows = jnp.concatenate([slot_rows, code_cols.astype(jnp.bfloat16)], axis=1)
    got = lax.all_to_all(out_rows, CACHE + ("mp",), split_axis=0, concat_axis=0, tiled=True)
    got_code = got[:, width].astype(jnp.int32) * CODE_BASE + got[:, width + 1].astype(jnp.int32)
    local_row = got_code - 1
    write_table = jnp.arange(rows_own, dtype=jnp.int32)[:, None] == local_row[None, :]
    placed = jnp.dot(
        write_table.astype(jnp.bfloat16), got[:, :width], preferred_element_type=jnp.float32
    ).astype(jnp.bfloat16)
    written = jnp.any(write_table, axis=1)
    fresh_cache = jnp.where(written[:, None], placed, stale_cache)
    local_blocks = rows_own // BLOCK
    block_count = local_blocks * device_count
    query_count, neg_count = neg_blocks.shape
    pair_count = query_count * neg_count
    query_cap = max(2, 2 * pair_count // block_count)
    pair_blocks = neg_blocks.reshape(-1)
    pair_marks = (pair_blocks[:, None] == jnp.arange(block_count, dtype=jnp.int32)[None, :]).astype(
        jnp.int32
    )
    pair_rank = jnp.sum(pair_marks * (jnp.cumsum(pair_marks, axis=0) - 1), axis=1)
    pair_slots = pair_blocks * query_cap + pair_rank
    pair_match = pair_slots[:, None] == jnp.arange(block_count * query_cap, dtype=jnp.int32)[None, :]
    slot_query = jnp.any(pair_match.reshape(query_count, neg_count, -1), axis=1)
    outbound = jnp.dot(
        slot_query.T.astype(jnp.bfloat16), queries, preferred_element_type=jnp.float32
    ).astype(jnp.bfloat16)
    arrived = lax.all_to_all(outbound, CACHE + ("mp",), split_axis=0, concat_axis=0, tiled=True)
    arrived = arrived.reshape(device_count, local_blocks, query_cap, width)
    block_keys = fresh_cache.reshape(local_blocks, BLOCK, width)
    scores = (
        jnp.einsum("snkd,nrd->snkr", arrived, block_keys, preferred_element_type=jnp.float32)
        * logit_scale
    )
    block_peak = jnp.max(scores, axis=-1)
    exp_terms = jnp.exp(scores - block_peak[..., None])
    block_total = jnp.sum(exp_terms, axis=-1)
    weights = exp_terms.astype(jnp.bfloat16)
    mixture = jnp.einsum("snkr,nrd->snkd", weights, block_keys, preferred_element_type=jnp.float32)
    packed = jnp.concatenate(
        [mixture.astype(jnp.bfloat16), split_parts(block_peak, block_total, width)], axis=-1
    )
    back = lax.all_to_all(
        packed.reshape(-1, packed.shape[-1]), CACHE + ("mp",), split_axis=0, concat_axis=0, tiled=True
    )
    pair_back = jnp.dot(
        pair_match.astype(jnp.bfloat16), back, preferred_element_type=jnp.float32
    )
    pair_mix = pair_back[:, :width].reshape(query_count, neg_count, width)
    pair_peak = join_parts(pair_back[:, width : width + 3]).reshape(query_count, neg_count)
    pair_total = join_parts(pair_back[:, width + 3 : width + 6]).reshape(query_count, neg_count)
    pick_table = (positive_ids[:, None] == jnp.arange(docs_here, dtype=jnp.int32)[None, :]).astype(
        jnp.bfloat16
    )
    positive = jnp.dot(pick_table, embedded, preferred_element_type=jnp.float32).astype(
        jnp.bfloat16
    )
    positive_f = positive.astype(jnp.float32)
    positive_logit = jnp.sum(queries.astype(jnp.float32) * positive_f, axis=-1) * logit_scale
    top_value = jnp.maximum(jnp.max(pair_peak, axis=-1), positive_logit)
    block_weight = jnp.exp(pair_peak - top_value[:, None])
    positive_weight = jnp.exp(positive_logit - top_value)
    partition = jnp.sum(block_weight * pair_total, axis=-1) + positive_weight
    loss = top_value + jnp.log(partition) - positive_logit
    pulled = (
        jnp.einsum("qn,qnd->qd", block_weight, pair_mix) + positive_weight[:, None] * positive_f
    )
    query_grad = logit_scale * (pulled / partition[:, None] - positive_f)
    return (fresh_cache, loss, query_grad)


def solution(mesh):
    placed = (
        P(CACHE + ("mp",), None),
        P(None, "mp"),
        P("mp", None),
        P(),
        P(),
        P(CACHE + ("mp",), None),
        P(CACHE + ("mp",)),
        P(CACHE + ("mp",), None),
        P(CACHE + ("mp",), None),
        P(CACHE + ("mp",)),
    )
    core_count = 2
    split_mesh = Mesh(
        mesh.devices.reshape(mesh.shape["cache"] // core_count, core_count, mesh.shape["mp"]),
        ("chip", "core", "mp"),
    )
    return jax.shard_map(
        shards,
        mesh=split_mesh,
        in_specs=placed,
        out_specs=(P(CACHE + ("mp",), None), P(CACHE + ("mp",)), P(CACHE + ("mp",), None)),
        check_vma=False,
    )
```

```python
import jax
import jax.numpy as jnp
from jax import lax
from jax.sharding import Mesh, PartitionSpec as P

D = 768
BLOCK = 128


epsilon = 1e-06
CACHE = ("chip", "core")
CODE_BASE = 32


def norm_rows(values):
    values = values.astype(jnp.float32)
    return values * lax.rsqrt(jnp.mean(values * values, axis=-1, keepdims=True) + epsilon)


def bf16_part(values):
    return lax.reduce_precision(values, exponent_bits=8, mantissa_bits=7)


def split_parts(peak, total, width):
    parts = []
    for values in (peak, total):
        high = bf16_part(values)
        rest = values - high
        middle = bf16_part(rest)
        parts += [high, middle, rest - middle]
    return jnp.stack(parts, axis=-1).astype(jnp.bfloat16)


def join_parts(parts):
    return (parts[:, 0] + parts[:, 1]) + parts[:, 2]


def shards(
    tokens,
    w_in,
    w_out,
    gain_in,
    gain_out,
    stale_cache,
    refresh_ids,
    queries,
    neg_blocks,
    positive_ids,
):
    cache_count = lax.axis_size(CACHE)
    mp_count = lax.axis_size("mp")
    docs_here = refresh_ids.shape[0]
    tok_rows = tokens.shape[0]
    doc_len = tok_rows // docs_here
    width = tokens.shape[1]
    logit_scale = D ** (-0.5)
    normed = (norm_rows(tokens) * gain_in).astype(jnp.bfloat16)
    piece_count = cache_count
    piece_rows = w_out.shape[0] // piece_count
    piece_at = lax.axis_index(CACHE) * piece_rows
    mp_here = lax.axis_index("mp")
    own_piece = lax.dynamic_slice_in_dim(w_out, piece_at, piece_rows, axis=0)
    mp_pieces = lax.all_to_all(
        jnp.broadcast_to(own_piece[None], (mp_count,) + own_piece.shape),
        "mp",
        split_axis=0,
        concat_axis=0,
        tiled=True,
    )
    normed, mp_pieces = lax.optimization_barrier((normed, mp_pieces))
    mp_twice = jnp.concatenate([mp_pieces, mp_pieces], axis=0)
    other_pieces = lax.dynamic_slice_in_dim(mp_twice, mp_here + 1, mp_count - 1, axis=0)
    rest_pieces = lax.all_to_all(
        jnp.broadcast_to(other_pieces[:, None], (mp_count - 1, piece_count) + own_piece.shape),
        CACHE,
        split_axis=1,
        concat_axis=1,
        tiled=True,
    )
    w_out_rest = rest_pieces.reshape(-1, width)
    w_in_full = lax.all_gather(w_in, "mp", axis=1, tiled=True)
    shard_cols = w_in.shape[1]
    w_in_rest = lax.dynamic_slice_in_dim(
        jnp.concatenate([w_in_full, w_in_full], axis=1),
        (mp_here + 1) * shard_cols,
        (mp_count - 1) * shard_cols,
        axis=1,
    )
    hidden_own = jnp.maximum(
        jnp.dot(normed, w_in, preferred_element_type=jnp.float32), 0.0
    ).astype(jnp.bfloat16)
    hidden_rest = jnp.maximum(
        jnp.dot(normed, w_in_rest, preferred_element_type=jnp.float32), 0.0
    ).astype(jnp.bfloat16)
    mixed = jnp.dot(hidden_own, w_out, preferred_element_type=jnp.float32) + jnp.dot(
        hidden_rest, w_out_rest, preferred_element_type=jnp.float32
    )
    state_sum = tokens.astype(jnp.float32) + mixed
    final_rows = norm_rows(state_sum) * gain_out
    pooled = jnp.mean(final_rows.reshape(docs_here, doc_len, width), axis=1)
    embedded = norm_rows(pooled).astype(jnp.bfloat16)
    rows_own = stale_cache.shape[0]
    device_count = cache_count * mp_count
    refresh_cap = 2 * docs_here // cache_count
    dest_of = refresh_ids // rows_own
    dest_hits = (dest_of[:, None] == jnp.arange(device_count, dtype=jnp.int32)[None, :]).astype(
        jnp.int32
    )
    rank_in = jnp.sum(dest_hits * (jnp.cumsum(dest_hits, axis=0) - 1), axis=1)
    slot_of = dest_of * refresh_cap + rank_in
    slot_match = slot_of[:, None] == jnp.arange(device_count * refresh_cap, dtype=jnp.int32)[None, :]
    code = jnp.sum(
        jnp.where(slot_match, (refresh_ids % rows_own + 1)[:, None], 0), axis=0
    )
    code_cols = jnp.zeros((code.shape[0], 128), jnp.float32)
    code_cols = code_cols.at[:, 0].set((code // CODE_BASE).astype(jnp.float32))
    code_cols = code_cols.at[:, 1].set((code % CODE_BASE).astype(jnp.float32))
    slot_rows = jnp.dot(
        slot_match.T.astype(jnp.bfloat16), embedded, preferred_element_type=jnp.float32
    ).astype(jnp.bfloat16)
    out_rows = jnp.concatenate([slot_rows, code_cols.astype(jnp.bfloat16)], axis=1)
    got = lax.all_to_all(out_rows, CACHE + ("mp",), split_axis=0, concat_axis=0, tiled=True)
    got_code = got[:, width].astype(jnp.int32) * CODE_BASE + got[:, width + 1].astype(jnp.int32)
    local_row = got_code - 1
    write_table = jnp.arange(rows_own, dtype=jnp.int32)[:, None] == local_row[None, :]
    placed = jnp.dot(
        write_table.astype(jnp.bfloat16), got[:, :width], preferred_element_type=jnp.float32
    ).astype(jnp.bfloat16)
    written = jnp.any(write_table, axis=1)
    fresh_cache = jnp.where(written[:, None], placed, stale_cache)
    local_blocks = rows_own // BLOCK
    block_count = local_blocks * device_count
    query_count, neg_count = neg_blocks.shape
    pair_count = query_count * neg_count
    query_cap = max(2, 2 * pair_count // block_count)
    pair_blocks = neg_blocks.reshape(-1)
    pair_marks = (pair_blocks[:, None] == jnp.arange(block_count, dtype=jnp.int32)[None, :]).astype(
        jnp.int32
    )
    pair_rank = jnp.sum(pair_marks * (jnp.cumsum(pair_marks, axis=0) - 1), axis=1)
    pair_slots = pair_blocks * query_cap + pair_rank
    pair_match = pair_slots[:, None] == jnp.arange(block_count * query_cap, dtype=jnp.int32)[None, :]
    slot_query = jnp.any(pair_match.reshape(query_count, neg_count, -1), axis=1)
    outbound = jnp.dot(
        slot_query.T.astype(jnp.bfloat16), queries, preferred_element_type=jnp.float32
    ).astype(jnp.bfloat16)
    arrived = lax.all_to_all(outbound, CACHE + ("mp",), split_axis=0, concat_axis=0, tiled=True)
    arrived = arrived.reshape(device_count, local_blocks, query_cap, width)
    block_keys = fresh_cache.reshape(local_blocks, BLOCK, width)
    scores = (
        jnp.einsum("snkd,nrd->snkr", arrived, block_keys, preferred_element_type=jnp.float32)
        * logit_scale
    )
    block_peak = jnp.max(scores, axis=-1)
    exp_terms = jnp.exp(scores - block_peak[..., None])
    block_total = jnp.sum(exp_terms, axis=-1)
    weights = exp_terms.astype(jnp.bfloat16)
    mixture = jnp.einsum("snkr,nrd->snkd", weights, block_keys, preferred_element_type=jnp.float32)
    dest_count = mixture.shape[0]
    slot_mix = mixture.astype(jnp.bfloat16).reshape(dest_count, -1, width)
    slots_per = slot_mix.shape[1]
    parts_row = split_parts(block_peak, block_total, width).reshape(dest_count, -1)
    part_cols = parts_row.shape[1]
    parts_row = jnp.pad(parts_row, [(0, 0), (0, width - part_cols)])
    packed = jnp.concatenate([slot_mix, parts_row[:, None]], axis=1)
    back = lax.all_to_all(packed, CACHE + ("mp",), split_axis=0, concat_axis=0, tiled=True)
    back_mix = back[:, :slots_per].reshape(-1, width)
    back_parts = back[:, slots_per, :part_cols].reshape(dest_count * slots_per, -1)
    pick = pair_match.astype(jnp.bfloat16)
    pair_mix = jnp.dot(pick, back_mix, preferred_element_type=jnp.float32).reshape(
        query_count, neg_count, width
    )
    pair_parts = jnp.dot(pick, back_parts, preferred_element_type=jnp.float32)
    pair_peak = join_parts(pair_parts[:, 0:3]).reshape(query_count, neg_count)
    pair_total = join_parts(pair_parts[:, 3:6]).reshape(query_count, neg_count)
    pick_table = (positive_ids[:, None] == jnp.arange(docs_here, dtype=jnp.int32)[None, :]).astype(
        jnp.bfloat16
    )
    positive = jnp.dot(pick_table, embedded, preferred_element_type=jnp.float32).astype(
        jnp.bfloat16
    )
    positive_f = positive.astype(jnp.float32)
    positive_logit = jnp.sum(queries.astype(jnp.float32) * positive_f, axis=-1) * logit_scale
    top_value = jnp.maximum(jnp.max(pair_peak, axis=-1), positive_logit)
    block_weight = jnp.exp(pair_peak - top_value[:, None])
    positive_weight = jnp.exp(positive_logit - top_value)
    partition = jnp.sum(block_weight * pair_total, axis=-1) + positive_weight
    loss = top_value + jnp.log(partition) - positive_logit
    pulled = (
        jnp.einsum("qn,qnd->qd", block_weight, pair_mix) + positive_weight[:, None] * positive_f
    )
    query_grad = logit_scale * (pulled / partition[:, None] - positive_f)
    return (fresh_cache, loss, query_grad)


def solution(mesh):
    placed = (
        P(CACHE + ("mp",), None),
        P(None, "mp"),
        P("mp", None),
        P(),
        P(),
        P(CACHE + ("mp",), None),
        P(CACHE + ("mp",)),
        P(CACHE + ("mp",), None),
        P(CACHE + ("mp",), None),
        P(CACHE + ("mp",)),
    )
    core_count = 2
    split_mesh = Mesh(
        mesh.devices.reshape(mesh.shape["cache"] // core_count, core_count, mesh.shape["mp"]),
        ("chip", "core", "mp"),
    )
    return jax.shard_map(
        shards,
        mesh=split_mesh,
        in_specs=placed,
        out_specs=(P(CACHE + ("mp",), None), P(CACHE + ("mp",)), P(CACHE + ("mp",), None)),
        check_vma=False,
    )
```

```python
import jax
import jax.numpy as jnp
from jax import lax
from jax.sharding import Mesh, PartitionSpec as P

D = 768
BLOCK = 128


epsilon = 1e-06
CACHE = ("chip", "core")
CODE_BASE = 32


def norm_rows(values):
    values = values.astype(jnp.float32)
    return values * lax.rsqrt(jnp.mean(values * values, axis=-1, keepdims=True) + epsilon)


def bf16_part(values):
    return lax.reduce_precision(values, exponent_bits=8, mantissa_bits=7)


def split_parts(peak, total, width):
    parts = []
    for values in (peak, total):
        high = bf16_part(values)
        rest = values - high
        middle = bf16_part(rest)
        parts += [high, middle, rest - middle]
    return jnp.stack(parts, axis=-1).astype(jnp.bfloat16)


def join_parts(parts):
    return (parts[:, 0] + parts[:, 1]) + parts[:, 2]


def shards(
    tokens,
    w_in,
    w_out,
    gain_in,
    gain_out,
    stale_cache,
    refresh_ids,
    queries,
    neg_blocks,
    positive_ids,
):
    cache_count = lax.axis_size(CACHE)
    mp_count = lax.axis_size("mp")
    docs_here = refresh_ids.shape[0]
    tok_rows = tokens.shape[0]
    doc_len = tok_rows // docs_here
    width = tokens.shape[1]
    logit_scale = D ** (-0.5)
    normed = (norm_rows(tokens) * gain_in).astype(jnp.bfloat16)
    piece_count = cache_count
    piece_rows = w_out.shape[0] // piece_count
    piece_at = lax.axis_index(CACHE) * piece_rows
    mp_here = lax.axis_index("mp")
    own_piece = lax.dynamic_slice_in_dim(w_out, piece_at, piece_rows, axis=0)
    mp_pieces = lax.all_to_all(
        jnp.broadcast_to(own_piece[None], (mp_count,) + own_piece.shape),
        "mp",
        split_axis=0,
        concat_axis=0,
        tiled=True,
    )
    normed, mp_pieces = lax.optimization_barrier((normed, mp_pieces))
    mp_twice = jnp.concatenate([mp_pieces, mp_pieces], axis=0)
    other_pieces = lax.dynamic_slice_in_dim(mp_twice, mp_here + 1, mp_count - 1, axis=0)
    rest_pieces = lax.all_to_all(
        jnp.broadcast_to(other_pieces[:, None], (mp_count - 1, piece_count) + own_piece.shape),
        CACHE,
        split_axis=1,
        concat_axis=1,
        tiled=True,
    )
    w_out_rest = rest_pieces.reshape(-1, width)
    w_in_full = lax.all_gather(w_in, "mp", axis=1, tiled=True)
    shard_cols = w_in.shape[1]
    w_in_rest = lax.dynamic_slice_in_dim(
        jnp.concatenate([w_in_full, w_in_full], axis=1),
        (mp_here + 1) * shard_cols,
        (mp_count - 1) * shard_cols,
        axis=1,
    )
    hidden_own = jnp.maximum(
        jnp.dot(normed, w_in, preferred_element_type=jnp.float32), 0.0
    ).astype(jnp.bfloat16)
    hidden_rest = jnp.maximum(
        jnp.dot(normed, w_in_rest, preferred_element_type=jnp.float32), 0.0
    ).astype(jnp.bfloat16)
    mixed = jnp.dot(hidden_own, w_out, preferred_element_type=jnp.float32) + jnp.dot(
        hidden_rest, w_out_rest, preferred_element_type=jnp.float32
    )
    state_sum = tokens.astype(jnp.float32) + mixed
    final_rows = norm_rows(state_sum) * gain_out
    pooled = jnp.mean(final_rows.reshape(docs_here, doc_len, width), axis=1)
    embedded = norm_rows(pooled).astype(jnp.bfloat16)
    rows_own = stale_cache.shape[0]
    device_count = cache_count * mp_count
    refresh_cap = 2 * docs_here // cache_count
    dest_of = refresh_ids // rows_own
    dest_hits = (dest_of[:, None] == jnp.arange(device_count, dtype=jnp.int32)[None, :]).astype(
        jnp.int32
    )
    rank_in = jnp.sum(dest_hits * (jnp.cumsum(dest_hits, axis=0) - 1), axis=1)
    slot_of = dest_of * refresh_cap + rank_in
    slot_match = slot_of[:, None] == jnp.arange(device_count * refresh_cap, dtype=jnp.int32)[None, :]
    code = jnp.sum(
        jnp.where(slot_match, (refresh_ids % rows_own + 1)[:, None], 0), axis=0
    )
    code_cols = jnp.zeros((code.shape[0], 128), jnp.float32)
    code_cols = code_cols.at[:, 0].set((code // CODE_BASE).astype(jnp.float32))
    code_cols = code_cols.at[:, 1].set((code % CODE_BASE).astype(jnp.float32))
    slot_rows = jnp.dot(
        slot_match.T.astype(jnp.bfloat16), embedded, preferred_element_type=jnp.float32
    ).astype(jnp.bfloat16)
    out_rows = jnp.concatenate([slot_rows, code_cols.astype(jnp.bfloat16)], axis=1)
    got = lax.all_to_all(out_rows, CACHE + ("mp",), split_axis=0, concat_axis=0, tiled=True)
    got_code = got[:, width].astype(jnp.int32) * CODE_BASE + got[:, width + 1].astype(jnp.int32)
    local_row = got_code - 1
    write_table = jnp.arange(rows_own, dtype=jnp.int32)[:, None] == local_row[None, :]
    placed = jnp.dot(
        write_table.astype(jnp.bfloat16), got[:, :width], preferred_element_type=jnp.float32
    ).astype(jnp.bfloat16)
    written = jnp.any(write_table, axis=1)
    fresh_cache = jnp.where(written[:, None], placed, stale_cache)
    local_blocks = rows_own // BLOCK
    block_count = local_blocks * device_count
    query_count, neg_count = neg_blocks.shape
    pair_count = query_count * neg_count
    query_cap = max(2, 2 * pair_count // block_count)
    pair_blocks = neg_blocks.reshape(-1)
    pair_marks = (pair_blocks[:, None] == jnp.arange(block_count, dtype=jnp.int32)[None, :]).astype(
        jnp.int32
    )
    pair_rank = jnp.sum(pair_marks * (jnp.cumsum(pair_marks, axis=0) - 1), axis=1)
    pair_slots = pair_blocks * query_cap + pair_rank
    pair_match = pair_slots[:, None] == jnp.arange(block_count * query_cap, dtype=jnp.int32)[None, :]
    slot_query = jnp.any(pair_match.reshape(query_count, neg_count, -1), axis=1)
    outbound = jnp.dot(
        slot_query.T.astype(jnp.bfloat16), queries, preferred_element_type=jnp.float32
    ).astype(jnp.bfloat16)
    arrived = lax.all_to_all(outbound, CACHE + ("mp",), split_axis=0, concat_axis=0, tiled=True)
    arrived = arrived.reshape(device_count, local_blocks, query_cap, width)
    block_keys = fresh_cache.reshape(local_blocks, BLOCK, width)
    scores = (
        jnp.einsum("snkd,nrd->snkr", arrived, block_keys, preferred_element_type=jnp.float32)
        * logit_scale
    )
    block_peak = jnp.max(scores, axis=-1)
    exp_terms = jnp.exp(scores - block_peak[..., None])
    block_total = jnp.sum(exp_terms, axis=-1)
    weights = exp_terms.astype(jnp.bfloat16)
    mixture = jnp.einsum("snkr,nrd->snkd", weights, block_keys, preferred_element_type=jnp.float32)
    dest_count = mixture.shape[0]
    slot_mix = mixture.astype(jnp.bfloat16).reshape(dest_count, -1)
    mix_cols = slot_mix.shape[1]
    parts_row = split_parts(block_peak, block_total, width).reshape(dest_count, -1)
    part_cols = parts_row.shape[1]
    parts_row = jnp.pad(parts_row, [(0, 0), (0, -part_cols % 128)])
    packed = jnp.concatenate([slot_mix, parts_row], axis=1)
    back = lax.all_to_all(packed, CACHE + ("mp",), split_axis=0, concat_axis=0, tiled=True)
    back_mix = back[:, :mix_cols].reshape(-1, width)
    back_parts = back[:, mix_cols : mix_cols + part_cols].reshape(back_mix.shape[0], -1)
    pick = pair_match.astype(jnp.bfloat16)
    pair_mix = jnp.dot(pick, back_mix, preferred_element_type=jnp.float32).reshape(
        query_count, neg_count, width
    )
    pair_parts = jnp.dot(pick, back_parts, preferred_element_type=jnp.float32)
    pair_peak = join_parts(pair_parts[:, 0:3]).reshape(query_count, neg_count)
    pair_total = join_parts(pair_parts[:, 3:6]).reshape(query_count, neg_count)
    pick_table = (positive_ids[:, None] == jnp.arange(docs_here, dtype=jnp.int32)[None, :]).astype(
        jnp.bfloat16
    )
    positive = jnp.dot(pick_table, embedded, preferred_element_type=jnp.float32).astype(
        jnp.bfloat16
    )
    positive_f = positive.astype(jnp.float32)
    positive_logit = jnp.sum(queries.astype(jnp.float32) * positive_f, axis=-1) * logit_scale
    top_value = jnp.maximum(jnp.max(pair_peak, axis=-1), positive_logit)
    block_weight = jnp.exp(pair_peak - top_value[:, None])
    positive_weight = jnp.exp(positive_logit - top_value)
    partition = jnp.sum(block_weight * pair_total, axis=-1) + positive_weight
    loss = top_value + jnp.log(partition) - positive_logit
    pulled = (
        jnp.einsum("qn,qnd->qd", block_weight, pair_mix) + positive_weight[:, None] * positive_f
    )
    query_grad = logit_scale * (pulled / partition[:, None] - positive_f)
    return (fresh_cache, loss, query_grad)


def solution(mesh):
    placed = (
        P(CACHE + ("mp",), None),
        P(None, "mp"),
        P("mp", None),
        P(),
        P(),
        P(CACHE + ("mp",), None),
        P(CACHE + ("mp",)),
        P(CACHE + ("mp",), None),
        P(CACHE + ("mp",), None),
        P(CACHE + ("mp",)),
    )
    core_count = 2
    split_mesh = Mesh(
        mesh.devices.reshape(mesh.shape["cache"] // core_count, core_count, mesh.shape["mp"]),
        ("chip", "core", "mp"),
    )
    return jax.shard_map(
        shards,
        mesh=split_mesh,
        in_specs=placed,
        out_specs=(P(CACHE + ("mp",), None), P(CACHE + ("mp",)), P(CACHE + ("mp",), None)),
        check_vma=False,
    )
```

```python
import jax
import jax.numpy as jnp
from jax import lax
from jax.sharding import Mesh, PartitionSpec as P

D = 768
BLOCK = 128


epsilon = 1e-06
CACHE = ("chip", "core")
CODE_BASE = 32


def norm_rows(values):
    values = values.astype(jnp.float32)
    return values * lax.rsqrt(jnp.mean(values * values, axis=-1, keepdims=True) + epsilon)


def bf16_part(values):
    return lax.reduce_precision(values, exponent_bits=8, mantissa_bits=7)


def split_parts(peak, total, width):
    parts = []
    for values in (peak, total):
        high = bf16_part(values)
        rest = values - high
        middle = bf16_part(rest)
        parts += [high, middle, rest - middle]
    pad = 128 - len(parts)
    stacked = jnp.stack(parts, axis=-1).astype(jnp.bfloat16)
    return jnp.pad(stacked, [(0, 0)] * (stacked.ndim - 1) + [(0, pad)])


def join_parts(parts):
    return (parts[:, 0] + parts[:, 1]) + parts[:, 2]


def shards(
    tokens,
    w_in,
    w_out,
    gain_in,
    gain_out,
    stale_cache,
    refresh_ids,
    queries,
    neg_blocks,
    positive_ids,
):
    cache_count = lax.axis_size(CACHE)
    mp_count = lax.axis_size("mp")
    docs_here = refresh_ids.shape[0]
    tok_rows = tokens.shape[0]
    doc_len = tok_rows // docs_here
    width = tokens.shape[1]
    logit_scale = D ** (-0.5)
    normed = (norm_rows(tokens) * gain_in).astype(jnp.bfloat16)
    piece_count = cache_count
    piece_rows = w_out.shape[0] // piece_count
    piece_at = lax.axis_index(CACHE) * piece_rows
    mp_here = lax.axis_index("mp")
    own_piece = lax.dynamic_slice_in_dim(w_out, piece_at, piece_rows, axis=0)
    mp_pieces = lax.all_to_all(
        jnp.broadcast_to(own_piece[None], (mp_count,) + own_piece.shape),
        "mp",
        split_axis=0,
        concat_axis=0,
        tiled=True,
    )
    normed, mp_pieces = lax.optimization_barrier((normed, mp_pieces))
    mp_twice = jnp.concatenate([mp_pieces, mp_pieces], axis=0)
    other_pieces = lax.dynamic_slice_in_dim(mp_twice, mp_here + 1, mp_count - 1, axis=0)
    rest_pieces = lax.all_to_all(
        jnp.broadcast_to(other_pieces[:, None], (mp_count - 1, piece_count) + own_piece.shape),
        CACHE,
        split_axis=1,
        concat_axis=1,
        tiled=True,
    )
    w_out_rest = rest_pieces.reshape(-1, width)
    w_in_full = lax.all_gather(w_in, "mp", axis=1, tiled=True)
    shard_cols = w_in.shape[1]
    w_in_rest = lax.dynamic_slice_in_dim(
        jnp.concatenate([w_in_full, w_in_full], axis=1),
        (mp_here + 1) * shard_cols,
        (mp_count - 1) * shard_cols,
        axis=1,
    )
    hidden_own = jnp.maximum(
        jnp.dot(normed, w_in, preferred_element_type=jnp.float32), 0.0
    ).astype(jnp.bfloat16)
    hidden_rest = jnp.maximum(
        jnp.dot(normed, w_in_rest, preferred_element_type=jnp.float32), 0.0
    ).astype(jnp.bfloat16)
    mixed = jnp.dot(hidden_own, w_out, preferred_element_type=jnp.float32) + jnp.dot(
        hidden_rest, w_out_rest, preferred_element_type=jnp.float32
    )
    state_sum = tokens.astype(jnp.float32) + mixed
    final_rows = norm_rows(state_sum) * gain_out
    pooled = jnp.mean(final_rows.reshape(docs_here, doc_len, width), axis=1)
    embedded = norm_rows(pooled).astype(jnp.bfloat16)
    rows_own = stale_cache.shape[0]
    device_count = cache_count * mp_count
    refresh_cap = 2 * docs_here // cache_count
    dest_of = refresh_ids // rows_own
    dest_hits = (dest_of[:, None] == jnp.arange(device_count, dtype=jnp.int32)[None, :]).astype(
        jnp.int32
    )
    rank_in = jnp.sum(dest_hits * (jnp.cumsum(dest_hits, axis=0) - 1), axis=1)
    slot_of = dest_of * refresh_cap + rank_in
    slot_match = slot_of[:, None] == jnp.arange(device_count * refresh_cap, dtype=jnp.int32)[None, :]
    code = jnp.sum(
        jnp.where(slot_match, (refresh_ids % rows_own + 1)[:, None], 0), axis=0
    )
    code_cols = jnp.zeros((code.shape[0], 128), jnp.float32)
    code_cols = code_cols.at[:, 0].set((code // CODE_BASE).astype(jnp.float32))
    code_cols = code_cols.at[:, 1].set((code % CODE_BASE).astype(jnp.float32))
    slot_rows = jnp.dot(
        slot_match.T.astype(jnp.bfloat16), embedded, preferred_element_type=jnp.float32
    ).astype(jnp.bfloat16)
    out_rows = jnp.concatenate([slot_rows, code_cols.astype(jnp.bfloat16)], axis=1)
    got = lax.all_to_all(out_rows, CACHE + ("mp",), split_axis=0, concat_axis=0, tiled=True)
    got_code = got[:, width].astype(jnp.int32) * CODE_BASE + got[:, width + 1].astype(jnp.int32)
    local_row = got_code - 1
    write_table = jnp.arange(rows_own, dtype=jnp.int32)[:, None] == local_row[None, :]
    placed = jnp.dot(
        write_table.astype(jnp.bfloat16), got[:, :width], preferred_element_type=jnp.float32
    ).astype(jnp.bfloat16)
    written = jnp.any(write_table, axis=1)
    fresh_cache = jnp.where(written[:, None], placed, stale_cache)
    local_blocks = rows_own // BLOCK
    block_count = local_blocks * device_count
    query_count, neg_count = neg_blocks.shape
    pair_count = query_count * neg_count
    query_cap = max(2, 2 * pair_count // block_count)
    pair_blocks = neg_blocks.reshape(-1)
    pair_marks = (pair_blocks[:, None] == jnp.arange(block_count, dtype=jnp.int32)[None, :]).astype(
        jnp.int32
    )
    pair_rank = jnp.sum(pair_marks * (jnp.cumsum(pair_marks, axis=0) - 1), axis=1)
    pair_slots = pair_blocks * query_cap + pair_rank
    pair_match = pair_slots[:, None] == jnp.arange(block_count * query_cap, dtype=jnp.int32)[None, :]
    slot_query = jnp.any(pair_match.reshape(query_count, neg_count, -1), axis=1)
    outbound = jnp.dot(
        slot_query.T.astype(jnp.bfloat16), queries, preferred_element_type=jnp.float32
    ).astype(jnp.bfloat16)
    arrived = lax.all_to_all(outbound, CACHE + ("mp",), split_axis=0, concat_axis=0, tiled=True)
    arrived = arrived.reshape(device_count, local_blocks, query_cap, width)
    block_keys = fresh_cache.reshape(local_blocks, BLOCK, width)
    scores = (
        jnp.einsum("snkd,nrd->snkr", arrived, block_keys, preferred_element_type=jnp.float32)
        * logit_scale
    )
    block_peak = jnp.max(scores, axis=-1)
    exp_terms = jnp.exp(scores - block_peak[..., None])
    block_total = jnp.sum(exp_terms, axis=-1)
    weights = exp_terms.astype(jnp.bfloat16)
    mixture = jnp.einsum("snkr,nrd->snkd", weights, block_keys, preferred_element_type=jnp.float32)
    packed = jnp.concatenate(
        [mixture.astype(jnp.bfloat16), split_parts(block_peak, block_total, width)], axis=-1
    )
    back = lax.all_to_all(
        packed.reshape(-1, packed.shape[-1]), CACHE + ("mp",), split_axis=0, concat_axis=0, tiled=True
    )
    pair_back = jnp.dot(
        pair_match.astype(jnp.bfloat16), back[:, width:], preferred_element_type=jnp.float32
    )
    pair_peak = join_parts(pair_back[:, 0:3]).reshape(query_count, neg_count)
    pair_total = join_parts(pair_back[:, 3:6]).reshape(query_count, neg_count)
    pick_table = (positive_ids[:, None] == jnp.arange(docs_here, dtype=jnp.int32)[None, :]).astype(
        jnp.bfloat16
    )
    positive = jnp.dot(pick_table, embedded, preferred_element_type=jnp.float32).astype(
        jnp.bfloat16
    )
    positive_f = positive.astype(jnp.float32)
    positive_logit = jnp.sum(queries.astype(jnp.float32) * positive_f, axis=-1) * logit_scale
    top_value = jnp.maximum(jnp.max(pair_peak, axis=-1), positive_logit)
    block_weight = jnp.exp(pair_peak - top_value[:, None])
    positive_weight = jnp.exp(positive_logit - top_value)
    partition = jnp.sum(block_weight * pair_total, axis=-1) + positive_weight
    loss = top_value + jnp.log(partition) - positive_logit
    slot_weight = jnp.sum(
        jnp.where(
            pair_match.reshape(query_count, neg_count, -1), block_weight[:, :, None], 0.0
        ),
        axis=1,
    )
    pulled = (
        jnp.dot(
            slot_weight,
            back[:, :width].astype(jnp.float32),
            precision=lax.Precision.HIGHEST,
            preferred_element_type=jnp.float32,
        )
        + positive_weight[:, None] * positive_f
    )
    query_grad = logit_scale * (pulled / partition[:, None] - positive_f)
    return (fresh_cache, loss, query_grad)


def solution(mesh):
    placed = (
        P(CACHE + ("mp",), None),
        P(None, "mp"),
        P("mp", None),
        P(),
        P(),
        P(CACHE + ("mp",), None),
        P(CACHE + ("mp",)),
        P(CACHE + ("mp",), None),
        P(CACHE + ("mp",), None),
        P(CACHE + ("mp",)),
    )
    core_count = 2
    split_mesh = Mesh(
        mesh.devices.reshape(mesh.shape["cache"] // core_count, core_count, mesh.shape["mp"]),
        ("chip", "core", "mp"),
    )
    return jax.shard_map(
        shards,
        mesh=split_mesh,
        in_specs=placed,
        out_specs=(P(CACHE + ("mp",), None), P(CACHE + ("mp",)), P(CACHE + ("mp",), None)),
        check_vma=False,
    )
```
